32 devices in a mesh: row: 4 (over z), col: 8 (over y, x, core).
Axes of the slice: x: 2, y: 2, z: 4, core: 2. Of those that a mesh axis runs over, the one named last changes fastest.
Arguments:
- load: float32 [4, 8, 640, 128], P('row', 'col'), may hold values from -16 to 16
- schur: float32 [4, 8, 640, 640], P('row', 'col'), may hold values from -0.090915483 to 4.0909155, as said below
- local_inverse: float32 [4, 8, 640, 640], P('row', 'col'), may hold values from -0.0059292706 to 0.30592927, as said below
- iface_index: int32 [4, 8, 640], P('row', 'col'), may hold values from 0 to 639, each once within a row
- face_link: int32 [4, 8, 4], P('row', 'col'), may hold values from 0 to 1, as said below
- coarse_basis: float32 [4, 8, 640, 48], P('row', 'col'), may hold values from -0.25 to 0.25
- coarse_inverse: float32 [8, 192, 192], P('col', 'row'), may hold values from -0.0036084392 to 0.06360844, as said below
- coarse_map: float32 [8, 192, 48], P('col', 'row'), may hold values from -0.875 to 0.875
- top_inverse: float32 [384, 384], P('col'), may hold values from -0.00025515518 to 0.006255155, as said below
Outputs:
- solution: float32 [4, 8, 640, 128], P('row', 'col')
- residual: float32 [4, 8, 640, 128], P('row', 'col')
The draws below stay inside these ranges and needn't reach their ends.
Inputs may be any that keep to these rules, and one draw needn't show every extreme that they name: `iface_index`: position j of face k of a subdomain and position j of the opposite face of its neighbour across face k are the same unknown. `face_link`: equal on the two sides of every face; 0 on faces on the outside of the grid of subdomains. `schur`: each matrix is symmetric. `local_inverse`: each matrix is symmetric. `coarse_inverse`: each matrix is symmetric. `top_inverse`: Symmetric.
All inputs are finite; a program needn't handle non-finite values.
Results may differ from the reference program's by a relative error of at most 0.0003.
Values sent between devices are 32-bit elements; how exact they have to be, the bound alone decides.
No kernel may reach another device: no remote copies, remote signals or barrier semaphores. Data moves between devices by JAX's collectives and lax.ppermute only.
A program may use at most 64 MiB of HBM per device.

```python
import math
import jax
import jax.numpy as jnp
from jax import lax

G = 640
R = 128
NC = 48
NT = 48
DEGREE = 2
STEPS = 4
MG = 192
MT = 384
N_ROW = 4
N_COL = 8


def symmetric_noise(key, shape):
    noise = jnp.clip(jax.random.normal(key, shape, jnp.float32), -4.0, 4.0)
    return (noise + jnp.swapaxes(noise, -1, -2)) * 0.5 ** 0.5


def stiffness_pair(key):
    uniform_diag = jax.random.uniform(jax.random.fold_in(key, 21), (N_ROW, N_COL, G), jnp.float32)
    diagonal = jnp.exp(uniform_diag * jnp.log(4.0))
    identity = jnp.eye(G, dtype=jnp.float32)
    noise_schur = symmetric_noise(jax.random.fold_in(key, 22), (N_ROW, N_COL, G, G))
    schur_part = identity * diagonal[..., None, :] + 0.4 / G ** 0.5 * noise_schur
    gain_part = 1.0 + 0.2 * jax.random.uniform(jax.random.fold_in(key, 23), (N_ROW, N_COL, G), jnp.float32, -1.0, 1.0)
    noise_local = symmetric_noise(jax.random.fold_in(key, 24), (N_ROW, N_COL, G, G))
    local_part = identity * (0.25 * gain_part / diagonal)[..., None, :] + 0.025 / G ** 0.5 * noise_local
    return (schur_part, local_part)


def draw_schur(key, part):
    return stiffness_pair(key)[0]


def draw_local_inverse(key, part):
    return stiffness_pair(key)[1]


def definite_draw(key, lead, order, lower, upper, spread):
    uniform_diag = jax.random.uniform(jax.random.fold_in(key, 31), lead + (order,), jnp.float32)
    diagonal = lower * jnp.exp(uniform_diag * jnp.log(upper / lower))
    noise = symmetric_noise(jax.random.fold_in(key, 32), lead + (order, order))
    return jnp.eye(order, dtype=jnp.float32) * diagonal[..., None, :] + spread / order ** 0.5 * noise


def draw_coarse_inverse(key, part):
    return definite_draw(key, (N_COL,), MG, 0.02, 0.06, 0.008)


def draw_top_inverse(key, part):
    return definite_draw(key, (), MT, 0.002, 0.006, 0.0008)


def draw_face_link(key, part):
    across = (jax.random.randint(jax.random.fold_in(key, 11), (N_ROW, N_COL - 1), 0, 8) > 0).astype(jnp.int32)
    upward = (jax.random.randint(jax.random.fold_in(key, 12), (N_ROW - 1, N_COL), 0, 8) > 0).astype(jnp.int32)
    blank_col = jnp.zeros((N_ROW, 1), jnp.int32)
    blank_row = jnp.zeros((1, N_COL), jnp.int32)
    west = jnp.concatenate([blank_col, across], axis=1)
    east = jnp.concatenate([across, blank_col], axis=1)
    south = jnp.concatenate([blank_row, upward], axis=0)
    north = jnp.concatenate([upward, blank_row], axis=0)
    return jnp.stack([west, east, south, north], axis=-1)


def level_of(key, dims, split, low, high):
    level = 1.0
    for position, parts in split:
        heights = jax.random.uniform(jax.random.fold_in(jax.random.fold_in(key, 6), position), (parts,), jnp.float32, low / len(split), high / len(split))
        level = level * jnp.repeat(jnp.exp(heights), dims[position] // parts).reshape((-1,) + (1,) * (len(dims) - 1 - position))
    return level


def scatter_about(rng, shape, scale, most, split=(), kind=jnp.bfloat16):
    loudness = level_of(rng, shape, split, -0.22, 0.18) if split else 1.0
    array = jax.random.normal(rng, shape, jnp.float32) * scale * loudness
    return jnp.minimum(jnp.maximum(array, -most), most).astype(kind)


def setup_inputs(seed: int = 0) -> dict:
    arg_keys = jax.random.split(jax.random.key(seed), 10)
    load = scatter_about(arg_keys[0], (N_ROW, N_COL, G, R), 4.0, 16.0, ((0, 4), (1, 8)), jnp.float32)
    schur = draw_schur(jax.random.fold_in(arg_keys[9], 71), 0)
    local_inverse = draw_local_inverse(jax.random.fold_in(arg_keys[9], 71), 0)
    iface_index = jax.vmap(lambda own: jax.random.permutation(own, G))(jax.random.split(arg_keys[3], N_ROW * N_COL)).reshape((N_ROW, N_COL, G)).astype(jnp.int32)
    face_link = draw_face_link(jax.random.fold_in(arg_keys[9], 71), 0)
    coarse_basis = scatter_about(arg_keys[5], (N_ROW, N_COL, G, NC), G ** -0.5, 0.25, ((0, 4), (1, 8)), jnp.float32)
    coarse_inverse = draw_coarse_inverse(jax.random.fold_in(arg_keys[9], 71), 0)
    coarse_map = scatter_about(arg_keys[7], (N_COL, MG, NT), NT ** -0.5, 0.875, ((0, 8), (1, 4)), jnp.float32)
    top_inverse = draw_top_inverse(jax.random.fold_in(arg_keys[9], 71), 0)
    return dict(load=load, schur=schur, local_inverse=local_inverse, iface_index=iface_index, face_link=face_link, coarse_basis=coarse_basis, coarse_inverse=coarse_inverse, coarse_map=coarse_map, top_inverse=top_inverse)


def assemble(field, iface_index, face_link):
    face_size = G // 4
    face_rows = jnp.take_along_axis(field, iface_index[..., None], axis=2)
    face_rows = face_rows.reshape(N_ROW, N_COL, 4, face_size, R)
    blank_col = jnp.zeros((N_ROW, 1, face_size, R), jnp.float32)
    blank_row = jnp.zeros((1, N_COL, face_size, R), jnp.float32)
    west = jnp.concatenate([blank_col, face_rows[:, :-1, 1]], axis=1)
    east = jnp.concatenate([face_rows[:, 1:, 0], blank_col], axis=1)
    south = jnp.concatenate([blank_row, face_rows[:-1, :, 3]], axis=0)
    north = jnp.concatenate([face_rows[1:, :, 2], blank_row], axis=0)
    received = jnp.stack([west, east, south, north], axis=2)
    received = received * face_link.astype(jnp.float32)[..., None, None]
    received = received.reshape(N_ROW, N_COL, G, R)

    def add_back(target, extra, index_list):
        return target.at[index_list].add(extra)

    return jax.vmap(jax.vmap(add_back))(field, received, iface_index)


def precondition(current, local_inverse, iface_index, face_link, coarse_basis, coarse_inverse, coarse_map, top_inverse):
    highest = lax.Precision.HIGHEST
    coeffs = jnp.einsum('abgk,abgr->abkr', coarse_basis, current, precision=highest)
    stacked = coeffs.transpose(1, 0, 2, 3).reshape(N_COL, MG, R)
    level_two = jnp.einsum('bij,bjr->bir', coarse_inverse, stacked, precision=highest)
    level_three = jnp.einsum('bik,bir->bkr', coarse_map, stacked, precision=highest)
    top = jnp.dot(top_inverse, level_three.reshape(MT, R), precision=highest, preferred_element_type=jnp.float32)
    group = level_two + jnp.einsum('bik,bkr->bir', coarse_map, top.reshape(N_COL, NT, R), precision=highest)
    group = group.reshape(N_COL, N_ROW, NC, R).transpose(1, 0, 2, 3)
    local = jnp.einsum('abij,abjr->abir', local_inverse, current, precision=highest)
    local = local + jnp.einsum('abgk,abkr->abgr', coarse_basis, group, precision=highest)
    return assemble(local, iface_index, face_link)


def reference(load, schur, local_inverse, iface_index, face_link, coarse_basis, coarse_inverse, coarse_map, top_inverse):
    highest = lax.Precision.HIGHEST
    assembled = assemble(load, iface_index, face_link)
    solution = jnp.zeros_like(load)
    for step_index in range(STEPS):
        phase = step_index % DEGREE
        weight_step = 1.0 / (1.4 - math.cos(math.pi * (2 * phase + 1) / (2 * DEGREE)))
        if step_index == 0:
            current = assembled
        else:
            applied = jnp.einsum('abij,abjr->abir', schur, solution, precision=highest)
            current = assembled - assemble(applied, iface_index, face_link)
        update = precondition(current, local_inverse, iface_index, face_link, coarse_basis, coarse_inverse, coarse_map, top_inverse)
        solution = solution + weight_step * update
    applied = jnp.einsum('abij,abjr->abir', schur, solution, precision=highest)
    residual = assembled - assemble(applied, iface_index, face_link)
    return solution, residual
```

```python
import functools
import math

import jax
import jax.numpy as jnp
from jax import lax
from jax.experimental import pallas as pl
from jax.experimental.pallas import tpu as pltpu
from jax.sharding import PartitionSpec as P

DEGREE = 2
STEPS = 4
LANES = 128
INTERPRET = False
F32 = jnp.float32
BF16 = jnp.bfloat16


def split(x, parts):
    pieces = []
    for _ in range(parts - 1):
        piece = x.astype(BF16)
        pieces.append(piece)
        x = x - piece.astype(F32)
    pieces.append(x.astype(BF16))
    return pieces


def stack_split(x):
    return jnp.concatenate(split(x, 2), axis=0)


def dot(left, right):
    return jnp.dot(left, right, preferred_element_type=F32)


def product_parts(left2, right_parts):
    rows = left2.shape[0] // 2
    n = right_parts[0].shape[1]
    out = dot(left2, jnp.concatenate(right_parts, axis=1))
    out = out[:rows] + out[rows:]
    return out[:, :n] + out[:, n:]


def product(left2, right):
    return product_parts(left2, split(right, 2))


def permuted(onehot, x, parts=3):
    n = x.shape[1]
    out = dot(onehot, jnp.concatenate(split(x, parts), axis=1))
    total = out[:, (parts - 1) * n :]
    for i in reversed(range(parts - 1)):
        total = out[:, i * n : (i + 1) * n] + total
    return total


def call(body, out_shapes, scalars, arrays, flops=0, scratch=()):
    smem = pl.BlockSpec(memory_space=pltpu.SMEM)
    vmem = pl.BlockSpec(memory_space=pltpu.VMEM)
    moved = sum(a.size * a.dtype.itemsize for a in arrays)
    return pl.pallas_call(
        body,
        out_shape=[jax.ShapeDtypeStruct(s, d) for s, d in out_shapes],
        in_specs=[smem] * len(scalars) + [vmem] * len(arrays),
        out_specs=[vmem] * len(out_shapes),
        scratch_shapes=[pltpu.VMEM(shape, F32) for shape in scratch],
        compiler_params=pltpu.CompilerParams(vmem_limit_bytes=24 * 2**20),
        cost_estimate=pl.CostEstimate(flops=flops, bytes_accessed=moved, transcendentals=0),
        interpret=INTERPRET,
    )(*scalars, *arrays)


def start_kernel(row_ref, col_ref, load_ref, basis_ref, map_ref, perm_ref, back_ref, load_out, basis_out, coarse_out):
    size = perm_ref.shape[0]
    perm = jnp.where(row_ref[...] == lax.broadcasted_iota(jnp.int32, (size, size), 1), 1.0, 0.0).astype(BF16)
    back_ref[...] = jnp.where(
        col_ref[...] == lax.broadcasted_iota(jnp.int32, (size, size), 0), 1.0, 0.0
    ).astype(BF16)
    perm_ref[...] = perm
    load_out[...] = permuted(perm, load_ref[...])
    basis = permuted(perm, basis_ref[...])
    basis_out[...] = basis
    coarse_out[...] = product(stack_split(basis), map_ref[...])


def split_kernel(*refs):
    half = len(refs) // 2
    for x_ref, o_ref in zip(refs[:half], refs[half:]):
        o_ref[...] = stack_split(x_ref[...])


def stacked(*arrays):
    return call(split_kernel, [((2 * a.shape[0], a.shape[1]), BF16) for a in arrays], [], arrays)


def level_kernel(
    face,
    link_ref,
    basis_ref,
    inverse_ref,
    map_top_ref,
    top_ref,
    basis_g_ref,
    basis_h_ref,
    inverse_g_ref,
    inverse_h_ref,
    map_g_ref,
    map_h_ref,
    coarse_e_ref,
    coarse_f_ref,
    top_e_ref,
    top_f_ref,
    two_ref,
    top_out_ref,
):
    coarse = map_top_ref[...]
    basis = basis_ref[...]
    top = top_ref[...]
    link = [link_ref[i].astype(F32) for i in range(4)]
    basis_g, basis_h = basis_g_ref[...] * link[2], basis_h_ref[...] * link[3]
    two = product(stack_split(basis), inverse_ref[...])
    two_g = product(stack_split(basis_g), inverse_g_ref[...])
    two_h = product(stack_split(basis_h), inverse_h_ref[...])
    two = jnp.concatenate([two[: 2 * face], two[2 * face : 3 * face] + two_g, two[3 * face :] + two_h], axis=0)
    two_ref[...] = stack_split(two)
    coarse_g = product(stack_split(basis_g), map_g_ref[...])
    coarse_h = product(stack_split(basis_h), map_h_ref[...])
    coarse = jnp.concatenate(
        [coarse[: 2 * face], coarse[2 * face : 3 * face] + coarse_g, coarse[3 * face :] + coarse_h], axis=0
    )
    out = product(stack_split(coarse), top)
    out_e = product(stack_split(coarse_e_ref[...] * link[0]), top_e_ref[...])
    out_f = product(stack_split(coarse_f_ref[...] * link[1]), top_f_ref[...])
    out = jnp.concatenate([out[:face] + out_e, out[face : 2 * face] + out_f, out[2 * face :]], axis=0)
    top_out_ref[...] = stack_split(out)


def received(link_ref, refs):
    return jnp.concatenate([r[...] * link_ref[i].astype(F32) for i, r in enumerate(refs)], axis=0)


def assemble_kernel(link_ref, load_ref, r0, r1, r2, r3, out_ref):
    out_ref[...] = load_ref[...] + received(link_ref, (r0, r1, r2, r3))


def current_kernel(first, face, *refs):
    if first:
        asm_ref, basis_ref, map_ref, inverse_ref, perm_ref, back_ref = refs[:6]
        outs = refs[6:]
        current = asm_ref[...]
    else:
        link_ref = refs[0]
        f_ref, r0, r1, r2, r3, asm_ref, basis_ref, map_ref, inverse_ref, perm_ref, back_ref = refs[1:12]
        outs = refs[12:]
        current = asm_ref[...] - (f_ref[...] + received(link_ref, (r0, r1, r2, r3)))
    y_ref, g_ref, h_ref, c_ref = outs
    coarse = basis_ref.shape[0] // 2
    parts = split(current, 2)
    coeffs = product_parts(basis_ref[...], parts)
    moved = dot(back_ref[...], jnp.concatenate(parts, axis=1)).astype(BF16)
    n = current.shape[1]
    y = product_parts(inverse_ref[...], [moved[:, :n], moved[:, n:]])
    y = permuted(perm_ref[...], y)
    y_ref[...] = y
    third = product(map_ref[...], coeffs)
    c_ref[:coarse] = coeffs
    c_ref[coarse:] = third
    for ref, k in ((g_ref, 2), (h_ref, 3)):
        ref[:face] = y[k * face : (k + 1) * face]
        ref[face : face + coarse] = coeffs
        ref[face + coarse :] = third


def group_kernel(face, pieces, coarse, link_ref, order_ref, y_ref, g_ref, h_ref, two_ref, *refs):
    cs = refs[:pieces]
    y2_ref, e_ref, third_ref, stack_ref = refs[pieces:]
    third = None
    for i, c in enumerate(cs):
        start = c.shape[0] - 2 * coarse
        offset = pl.multiple_of(order_ref[i], 8)
        stack_ref[pl.ds(offset, coarse)] = c[start : start + coarse]
        part = c[start + coarse :]
        third = part if third is None else third + part
    y = y_ref[...] + product(two_ref[...], stack_ref[...])
    y2_ref[: 2 * face] = y[: 2 * face]
    y2_ref[2 * face : 3 * face] = y[2 * face : 3 * face] + g_ref[:face] * link_ref[2].astype(F32)
    y2_ref[3 * face :] = y[3 * face :] + h_ref[:face] * link_ref[3].astype(F32)
    e_ref[:face] = y[:face]
    e_ref[face:] = third
    third_ref[...] = third


def update_kernel(weight, first, face, starts, top, link_ref, order_ref, y2_ref, e_ref, f_ref, top_ref, perm_ref, back_ref, schur_ref, *refs):
    if not first:
        old_ref, refs = refs[0], refs[1:]
    x_ref, out_ref, stack_ref = refs[len(starts) :]
    slot = 0
    for ref, first_row in zip(refs, starts):
        for start in range(first_row, ref.shape[0], top):
            offset = pl.multiple_of(order_ref[slot], 8)
            stack_ref[pl.ds(offset, top)] = ref[start : start + top]
            slot += 1
    y2 = y2_ref[...] + product(top_ref[...], stack_ref[...])
    update = jnp.concatenate(
        [
            y2[:face] + e_ref[:face] * link_ref[0].astype(F32),
            y2[face : 2 * face] + f_ref[...] * link_ref[1].astype(F32),
            y2[2 * face :],
        ],
        axis=0,
    )
    x = weight * permuted(back_ref[...], update)
    if not first:
        x = old_ref[...] + x
    x_ref[...] = x
    out_ref[...] = permuted(perm_ref[...], product(schur_ref[...], x))


def residual_kernel(link_ref, f_ref, r0, r1, r2, r3, asm_ref, back_ref, out_ref):
    current = asm_ref[...] - (f_ref[...] + received(link_ref, (r0, r1, r2, r3)))
    out_ref[...] = permuted(back_ref[...], current)


def xor_pairs(count, bits):
    return [(i, i ^ bits) for i in range(count) if i ^ bits < count]


def odd_pairs(count):
    return [(i, i + 1 if i % 2 else i - 1) for i in range(count) if 0 <= (i + 1 if i % 2 else i - 1) < count]


def swap(x, axis, pairs):
    return lax.ppermute(x, axis, pairs)


def lanes(x):
    width = -(-x.shape[1] // LANES) * LANES
    x = jnp.pad(x, ((0, 0), (0, width - x.shape[1])))
    return jnp.concatenate([x[:, i : i + LANES] for i in range(0, width, LANES)], axis=0)


def unlanes(x, rows, columns):
    parts = [x[i : i + rows] for i in range(0, x.shape[0], rows)]
    return jnp.concatenate(parts, axis=1)[:, :columns]


def shards(
    load,
    schur,
    local_inverse,
    iface_index,
    face_link,
    coarse_basis,
    coarse_inverse,
    coarse_map,
    top_inverse,
):
    loads, basis = load[0, 0], coarse_basis[0, 0]
    inverse_rows, map_block = coarse_inverse[0], coarse_map[0]
    size, columns = loads.shape
    face = size // 4
    coarse, top = basis.shape[1], map_block.shape[1]
    rows, cols = lax.axis_size("row"), lax.axis_size("col")
    row, col = lax.axis_index("row"), lax.axis_index("col")
    width = top_inverse.shape[1]

    def by_partner(x):
        west, east, south, north = x
        even_col, even_row = col % 2 == 0, row % 2 == 0
        return [
            jnp.where(even_col, east, west),
            jnp.where(even_col, west, east),
            jnp.where(even_row, north, south),
            jnp.where(even_row, south, north),
        ]

    index = jnp.concatenate(by_partner(iface_index[0, 0].reshape(4, face)))
    link = jnp.stack(by_partner(face_link[0, 0]))

    col_even, col_odd = xor_pairs(cols, 1), odd_pairs(cols)
    row_even, row_odd = xor_pairs(rows, 1), odd_pairs(rows)
    ring = rows == 4
    if ring:
        row_odd = xor_pairs(rows, 3)
    doubling = cols & (cols - 1) == 0

    def exchange(parts):
        return [
            swap(parts[0], "col", col_even),
            swap(parts[1], "col", col_odd),
            swap(parts[2], "row", row_even),
            swap(parts[3], "row", row_odd),
        ]

    def faces(x):
        return [x[i * face : (i + 1) * face] for i in range(4)]

    n = (size, columns)
    perm, back, load_f, basis_f, coarse_f = call(
        start_kernel,
        [((size, size), BF16), ((size, size), BF16), (n, F32), ((size, coarse), F32), ((size, top), F32)],
        [],
        [index.reshape(size, 1), index.reshape(1, size), loads, basis, map_block],
        flops=4 * size**2 * columns,
    )
    schur2, inverse2 = stacked(schur[0, 0], local_inverse[0, 0])
    basis2, map2 = stacked(basis_f.T, map_block.T)

    along_col = lanes(top_inverse)
    along_row = jnp.concatenate([lanes(inverse_rows), lanes(map_block)])
    got = exchange(
        [jnp.concatenate([x, lanes(y), along_col]) for x, y in zip(faces(load_f)[:2], faces(coarse_f)[:2])]
        + [jnp.concatenate([x, lanes(y), along_row]) for x, y in zip(faces(load_f)[2:], faces(basis_f)[2:])]
    )
    assembled = call(assemble_kernel, [(n, F32)], [link], [load_f] + [g[:face] for g in got])[0]
    second = [g[face : 2 * face] for g in got]
    rest = [g[2 * face :] for g in got]
    split_at = lanes(inverse_rows).shape[0]
    total = rows * coarse
    two2, top2 = call(
        functools.partial(level_kernel, face),
        [((2 * size, total), BF16), ((2 * size, width), BF16)],
        [link],
        [basis_f, inverse_rows, coarse_f, top_inverse]
        + [second[2][:, :coarse], second[3][:, :coarse]]
        + [unlanes(rest[k][:split_at], coarse, total) for k in (2, 3)]
        + [unlanes(rest[k][split_at:], coarse, top) for k in (2, 3)]
        + [second[0][:, :top], second[1][:, :top]]
        + [unlanes(rest[k], top, width) for k in (0, 1)],
    )

    if ring:
        row_order = jnp.stack([(row ^ i) * coarse for i in range(rows)])
    else:
        row_order = jnp.arange(rows, dtype=jnp.int32) * coarse
    if doubling:
        col_order = jnp.stack([(col ^ i) * top for i in range(cols)])
    else:
        col_order = jnp.arange(cols, dtype=jnp.int32) * top

    solution, field = None, None
    square = 8 * size * size * columns
    for step_index in range(STEPS):
        phase = step_index % DEGREE
        weight = 1.0 / (1.4 - math.cos(math.pi * (2 * phase + 1) / (2 * DEGREE)))
        first = step_index == 0
        stationary = [assembled, basis2, map2, inverse2, perm, back]
        if first:
            head, scalars = [], []
        else:
            head, scalars = [field] + exchange(faces(field)), [link]
        y, pay_g, pay_h, coeffs = call(
            functools.partial(current_kernel, first, face),
            [
                (n, F32),
                ((face + coarse + top, columns), F32),
                ((face + coarse + top, columns), F32),
                ((coarse + top, columns), F32),
            ],
            scalars,
            head + stationary,
            flops=2 * square,
        )
        got_g = swap(pay_g, "row", row_even)
        got_h = swap(pay_h, "row", row_odd)
        if ring:
            got_r = swap(coeffs, "row", xor_pairs(rows, 2))
            pieces = [coeffs, got_g, got_r, got_h]
        else:
            everyone = lax.all_gather(coeffs, "row", axis=0)
            pieces = [everyone[i] for i in range(rows)]
        y2, pay_e, third = call(
            functools.partial(group_kernel, face, len(pieces), coarse),
            [(n, F32), ((face + top, columns), F32), ((top, columns), F32)],
            [link, row_order],
            [y, got_g, got_h, two2] + pieces,
            scratch=[(total, columns)],
        )
        got_e = swap(pay_e, "col", col_even)
        got_f = swap(y2[face : 2 * face], "col", col_odd)
        starts = [0]
        if doubling:
            tops = [third, got_e]
            starts = [0, face]
            known = jnp.concatenate([third, got_e[face:]])
            bits = 2
            while bits < cols:
                more = swap(known, "col", xor_pairs(cols, bits))
                tops.append(more)
                starts.append(0)
                known = jnp.concatenate([known, more])
                bits *= 2
        else:
            tops = [lax.all_gather(third, "col", axis=0, tiled=True)]
        solution, field = call(
            functools.partial(update_kernel, weight, first, face, starts, top),
            [(n, F32), (n, F32)],
            [link, col_order],
            [y2, got_e, got_f, top2, perm, back, schur2] + ([] if first else [solution]) + tops,
            flops=2 * square,
            scratch=[(width, columns)],
        )
    residual = call(
        residual_kernel,
        [(n, F32)],
        [link],
        [field] + exchange(faces(field)) + [assembled, back],
    )[0]
    return (solution[None, None], residual[None, None])


def solution(mesh):
    return jax.shard_map(
        shards,
        mesh=mesh,
        in_specs=(
            P("row", "col", None, None),
            P("row", "col", None, None),
            P("row", "col", None, None),
            P("row", "col", None),
            P("row", "col", None),
            P("row", "col", None, None),
            P("col", "row", None),
            P("col", "row", None),
            P("col", None),
        ),
        out_specs=(P("row", "col", None, None), P("row", "col", None, None)),
        check_vma=False,
    )
```

```python
import functools
import math

import jax
import jax.numpy as jnp
from jax import lax
from jax.experimental import pallas as pl
from jax.experimental.pallas import tpu as pltpu
from jax.sharding import PartitionSpec as P


DEGREE = 2
STEPS = 4
LANES = 128
INTERPRET = False
VMEM_LIMIT = 16 * 2**20
F32 = jnp.float32
BF16 = jnp.bfloat16


def split(x, parts):
    pieces = []
    for _ in range(parts - 1):
        piece = x.astype(BF16)
        pieces.append(piece)
        x = x - piece.astype(F32)
    pieces.append(x.astype(BF16))
    return pieces


def stack_split(x):
    return jnp.concatenate(split(x, 2), axis=0)


def dot(left, right):
    return jnp.dot(left, right, preferred_element_type=F32)


def product_parts(left2, right_parts):
    rows = left2.shape[0] // 2
    n = right_parts[0].shape[1]
    out = dot(left2, jnp.concatenate(right_parts, axis=1))
    out = out[:rows] + out[rows:]
    return out[:, :n] + out[:, n:]


def product(left2, right):
    return product_parts(left2, split(right, 2))


def permuted(onehot, x, parts=2):
    n = x.shape[1]
    out = dot(onehot, jnp.concatenate(split(x, parts), axis=1))
    total = out[:, (parts - 1) * n :]
    for i in reversed(range(parts - 1)):
        total = out[:, i * n : (i + 1) * n] + total
    return total


def call(body, out_shapes, scalars, arrays, flops=0, scratch=(), space=pltpu.VMEM):
    smem = pl.BlockSpec(memory_space=pltpu.SMEM)
    vmem = pl.BlockSpec(memory_space=pltpu.VMEM)
    moved = sum(a.size * a.dtype.itemsize for a in arrays)
    return pl.pallas_call(
        body,
        out_shape=[jax.ShapeDtypeStruct(s, d) for s, d in out_shapes],
        in_specs=[smem] * len(scalars) + [pl.BlockSpec(memory_space=space)] * len(arrays),
        out_specs=[vmem] * len(out_shapes),
        scratch_shapes=[pltpu.VMEM(shape, F32) if isinstance(shape, tuple) else shape for shape in scratch],
        compiler_params=pltpu.CompilerParams(vmem_limit_bytes=VMEM_LIMIT),
        cost_estimate=pl.CostEstimate(flops=flops, bytes_accessed=moved, transcendentals=0),
        interpret=INTERPRET,
    )(*scalars, *arrays)


def pack(ref, start, x):
    rows, width = x.shape
    for i in range(0, width, LANES):
        w = min(LANES, width - i)
        ref[start : start + rows, :w] = x[:, i : i + w]
        start += rows
    return start


def unpack(ref, start, rows, width):
    parts = []
    for i in range(0, width, LANES):
        parts.append(ref[start : start + rows, : min(LANES, width - i)])
        start += rows
    return jnp.concatenate(parts, axis=1) if len(parts) > 1 else parts[0]


def blocks(width):
    return -(-width // LANES)


def pack_halves(ref, start, x):
    half = x.shape[0] // 2
    ref[start : start + half, : x.shape[1]] = x[:half]
    ref[start : start + half, LANES // 2 : LANES // 2 + x.shape[1]] = x[half:]


def unpack_halves(ref, start, rows, width):
    x = ref[start : start + rows // 2, :]
    return jnp.concatenate([x[:, :width], x[:, LANES // 2 : LANES // 2 + width]], axis=0)


def transposed(x, pad_ref):
    rows, width = x.shape
    pad_ref[...] = jnp.zeros_like(pad_ref)
    pad_ref[:rows, :width] = x
    return pad_ref[...].T[:width, :rows]


def start_kernel(
    face,
    place_ref,
    index_hbm,
    load_hbm,
    basis_hbm,
    map_hbm,
    inverse_hbm,
    top_hbm,
    perm_ref,
    back_ref,
    load_out,
    basis_out,
    coarse_out,
    basis2_ref,
    map2_ref,
    map_t_ref,
    e_ref,
    f_ref,
    g_ref,
    h_ref,
    index_ref,
    load_ref,
    basis_ref,
    map_ref,
    inverse_ref,
    top_ref,
    tall_ref,
    small_ref,
    sems,
):
    sources = (index_hbm, load_hbm, basis_hbm, map_hbm, inverse_hbm, top_hbm)
    targets = (index_ref, load_ref, basis_ref, map_ref, inverse_ref, top_ref)
    copies = [pltpu.make_async_copy(a, b, sems.at[i]) for i, (a, b) in enumerate(zip(sources, targets))]
    for copy in copies:
        copy.start()
    size = perm_ref.shape[0]
    coarse = basis_ref.shape[1]
    for ref in (e_ref, f_ref, g_ref, h_ref):
        ref[face:] = jnp.zeros((ref.shape[0] - face, ref.shape[1]), F32)
    copies[0].wait()
    raw = index_ref[...].astype(F32)
    west, east, south, north = [raw[:, k * face : (k + 1) * face] for k in range(4)]
    even_row, even_col = place_ref[0] % 2 == 0, place_ref[1] % 2 == 0
    index = jnp.concatenate(
        [
            jnp.where(even_col, east, west),
            jnp.where(even_col, west, east),
            jnp.where(even_row, north, south),
            jnp.where(even_row, south, north),
        ],
        axis=1,
    )
    tall = jnp.broadcast_to(index, (LANES, size)).T
    lane = lax.broadcasted_iota(jnp.int32, (size, LANES), 1).astype(F32)
    for i in range(0, size, LANES):
        perm_ref[:, i : i + LANES] = jnp.where(tall == lane + float(i), 1.0, 0.0).astype(BF16)
    perm = perm_ref[...]
    copies[1].wait()
    load = permuted(perm, load_ref[...])
    load_out[...] = load
    for copy in copies[2:]:
        copy.wait()
    basis = permuted(perm, basis_ref[...])
    basis_out[...] = basis
    product_map = product(stack_split(basis), map_ref[...])
    coarse_out[...] = product_map
    level = jnp.concatenate([inverse_ref[...], map_ref[...]], axis=1)
    for k, ref in enumerate((e_ref, f_ref, g_ref, h_ref)):
        rows = slice(k * face, (k + 1) * face)
        ref[:face] = load[rows]
        pack_halves(ref, face, product_map[rows] if k < 2 else basis[rows])
        pack(ref, face + face // 2, top_ref[...] if k < 2 else level)
    down = lax.broadcasted_iota(jnp.int32, (size, size), 0).astype(F32)
    back_ref[...] = jnp.where(index == down, 1.0, 0.0).astype(BF16)
    basis2_ref[...] = stack_split(transposed(basis, tall_ref))
    map_t = transposed(map_ref[...], small_ref)
    map2_ref[...] = stack_split(map_t)
    map_t_ref[...] = jnp.zeros_like(map_t_ref)
    map_t_ref[:, :coarse] = map_t


def split_kernel(x_ref, o_ref):
    o_ref[...] = stack_split(x_ref[...])


def level_kernel(
    face, link_ref, basis_ref, inverse_ref, coarse_ref, top_ref, e_ref, f_ref, g_ref, h_ref, two_ref, top_out_ref
):
    coarse, total = inverse_ref.shape
    top, width = top_ref.shape
    start = face + face // 2
    link = [link_ref[i].astype(F32) for i in range(4)]
    two = product(stack_split(basis_ref[...]), inverse_ref[...])
    third = coarse_ref[...]
    twos, thirds = [two[: 2 * face]], [third[: 2 * face]]
    for k, ref in ((2, g_ref), (3, h_ref)):
        rows = slice(k * face, (k + 1) * face)
        basis = stack_split(unpack_halves(ref, face, face, coarse) * link[k])
        level = product(basis, unpack(ref, start, coarse, total + top))
        twos.append(two[rows] + level[:, :total])
        thirds.append(third[rows] + level[:, total:])
    two_ref[...] = stack_split(jnp.concatenate(twos, axis=0))
    out = product(stack_split(jnp.concatenate(thirds, axis=0)), top_ref[...])
    outs = []
    for k, ref in ((0, e_ref), (1, f_ref)):
        rows = slice(k * face, (k + 1) * face)
        near = stack_split(unpack_halves(ref, face, face, top) * link[k])
        outs.append(out[rows] + product(near, unpack(ref, start, top, width)))
    top_out_ref[...] = stack_split(jnp.concatenate(outs + [out[2 * face :]], axis=0))


def received(face, link_ref, refs):
    return jnp.concatenate([r[:face] * link_ref[i].astype(F32) for i, r in enumerate(refs)], axis=0)


def coeffs_kernel(first, face, link_ref, f_ref, r0, r1, r2, r3, *refs):
    field = f_ref[...] + received(face, link_ref, (r0, r1, r2, r3))
    if first:
        basis_ref, current_ref, c_ref = refs
        current = field
    else:
        asm_ref, basis_ref, current_ref, c_ref = refs
        current = asm_ref[...] - field
    current_ref[...] = current
    c_ref[...] = product(basis_ref[...], current)


def local_kernel(face, current_ref, inverse_ref, perm_ref, back_ref, y_ref, g_ref, h_ref):
    n = current_ref.shape[1]
    moved = dot(back_ref[...], jnp.concatenate(split(current_ref[...], 2), axis=1)).astype(BF16)
    y = permuted(perm_ref[...], product_parts(inverse_ref[...], [moved[:, :n], moved[:, n:]]))
    y_ref[...] = y
    g_ref[...] = y[2 * face : 3 * face]
    h_ref[...] = y[3 * face :]


def maps_kernel(coarse, starts, *refs):
    out_ref = refs[-1]
    slot = 0
    for ref, spans in zip(refs, starts):
        for start in spans:
            part = stack_split(ref[start : start + coarse, :coarse])
            out_ref[slot * part.shape[0] : (slot + 1) * part.shape[0]] = part
            slot += 1


def third_kernel(starts, coarse, maps_ref, *refs):
    third, slot = None, 0
    rows = maps_ref.shape[0] // sum(len(spans) for spans in starts)
    for ref, spans in zip(refs, starts):
        for start in spans:
            part = product(maps_ref[slot * rows : (slot + 1) * rows], ref[start : start + coarse])
            third = part if third is None else third + part
            slot += 1
    refs[-1][...] = third


def group_kernel(face, starts, coarse, link_ref, order_ref, y_ref, g_ref, h_ref, two_ref, *refs):
    y2_ref, stack_ref = refs[len(starts) :]
    slot = 0
    for ref, spans in zip(refs, starts):
        for start in spans:
            offset = pl.multiple_of(order_ref[slot], 8)
            stack_ref[pl.ds(offset, coarse)] = ref[start : start + coarse]
            slot += 1
    y = y_ref[...] + product(two_ref[...], stack_ref[...])
    y2_ref[: 2 * face] = y[: 2 * face]
    y2_ref[2 * face : 3 * face] = y[2 * face : 3 * face] + g_ref[:face] * link_ref[2].astype(F32)
    y2_ref[3 * face :] = y[3 * face :] + h_ref[:face] * link_ref[3].astype(F32)


def update_kernel(
    weight, first, face, starts, top, link_ref, order_ref, y2_ref, e_ref, f_ref, top_ref, perm_ref, back_ref, schur_ref, *refs
):
    if not first:
        old_ref, refs = refs[0], refs[1:]
    x_ref, out_ref, stack_ref = refs[len(starts) :]
    slot = 0
    for ref, first_row in zip(refs, starts):
        for start in range(first_row, ref.shape[0], top):
            stack_ref[pl.ds(pl.multiple_of(order_ref[slot], 8), top)] = ref[start : start + top]
            slot += 1
    y2 = y2_ref[...] + product(top_ref[...], stack_ref[...])
    update = jnp.concatenate(
        [
            y2[:face] + e_ref[:face] * link_ref[0].astype(F32),
            y2[face : 2 * face] + f_ref[:face] * link_ref[1].astype(F32),
            y2[2 * face :],
        ],
        axis=0,
    )
    x = weight * permuted(back_ref[...], update)
    if not first:
        x = old_ref[...] + x
    x_ref[...] = x
    out_ref[...] = permuted(perm_ref[...], product(schur_ref[...], x))


def residual_kernel(face, link_ref, f_ref, r0, r1, r2, r3, asm_ref, back_ref, out_ref):
    current = asm_ref[...] - (f_ref[...] + received(face, link_ref, (r0, r1, r2, r3)))
    out_ref[...] = permuted(back_ref[...], current, 3)


def swap_pairs(rows, cols, partner):
    pairs = []
    for r in range(rows):
        for c in range(cols):
            a, b = partner(r, c)
            if not (0 <= a < rows and 0 <= b < cols):
                a, b = (r, c ^ 1) if not 0 <= a < rows else (r ^ 1, c)
            if a < rows and b < cols:
                pairs.append((r * cols + c, a * cols + b))
    return pairs


def odd_neighbour(i):
    return i + 1 if i % 2 else i - 1


def shards(
    load,
    schur,
    local_inverse,
    iface_index,
    face_link,
    coarse_basis,
    coarse_inverse,
    coarse_map,
    top_inverse,
):
    loads, basis = load[0, 0], coarse_basis[0, 0]
    inverse_rows, map_block = coarse_inverse[0], coarse_map[0]
    size, columns = loads.shape
    face = size // 4
    coarse, top = basis.shape[1], map_block.shape[1]
    rows, cols = lax.axis_size("row"), lax.axis_size("col")
    row, col = lax.axis_index("row"), lax.axis_index("col")
    total, width = inverse_rows.shape[1], top_inverse.shape[1]

    place = jnp.stack([row, col])
    side = jnp.arange(4, dtype=jnp.int32)
    parity = jnp.where(side < 2, col, row) & 1
    facing = jnp.where(side < 2, 0, 2) + ((side & 1) ^ parity ^ 1)
    link = jnp.sum(jnp.where(facing[:, None] == side[None, :], face_link[0, 0][None, :], 0), axis=1)

    def swap(x, partner):
        return lax.ppermute(x, ("row", "col"), swap_pairs(rows, cols, partner))

    def swap_even_col(x):
        return swap(x, lambda r, c: (r, c ^ 1))

    def swap_odd_col(x):
        return swap(x, lambda r, c: (r, odd_neighbour(c)))

    def swap_even_row(x):
        return swap(x, lambda r, c: (r ^ 1, c))

    def swap_odd_row(x):
        return swap(x, lambda r, c: (odd_neighbour(r), c))

    def exchange(parts):
        got_f = swap_odd_col(parts[1])
        got_g = swap_even_row(parts[2])
        got_h = swap_odd_row(parts[3])
        got_e = swap_even_col(parts[0])
        return [got_e, got_f, got_g, got_h]

    row_pairs = rows == 4

    def faces(x):
        return [x[i * face : (i + 1) * face] for i in range(4)]

    n = (size, columns)
    common = face + face // 2
    payloads = [common + blocks(width) * top] * 2 + [common + blocks(total + top) * coarse] * 2
    perm, back, load_f, basis_f, coarse_f, basis2, map2, map_t, *sent = call(
        functools.partial(start_kernel, face),
        [((size, size), BF16), ((size, size), BF16), (n, F32), ((size, coarse), F32), ((size, top), F32)]
        + [((2 * coarse, size), BF16), ((2 * top, coarse), BF16), ((top, columns), F32)]
        + [((p, columns), F32) for p in payloads],
        [place],
        [iface_index[0], loads, basis, map_block, inverse_rows, top_inverse],
        flops=4 * size**2 * columns,
        scratch=[pltpu.VMEM((1, size), jnp.int32), n, basis.shape, map_block.shape, inverse_rows.shape]
        + [top_inverse.shape, (size, LANES), (LANES, LANES), pltpu.SemaphoreType.DMA((6,))],
        space=pltpu.HBM,
    )
    schur2 = call(split_kernel, [((2 * size, size), BF16)], [], [schur[0, 0]])[0]
    inverse2 = call(split_kernel, [((2 * size, size), BF16)], [], [local_inverse[0, 0]])[0]

    got = exchange(sent)
    two2, top2 = call(
        functools.partial(level_kernel, face),
        [((2 * size, total), BF16), ((2 * size, width), BF16)],
        [link],
        [basis_f, inverse_rows, coarse_f, top_inverse] + got,
    )

    doubling = cols & (cols - 1) == 0
    col_order = jnp.arange(cols, dtype=jnp.int32)
    if doubling:
        col_order = col_order ^ col
    col_order = col_order * top
    row_order = jnp.arange(rows, dtype=jnp.int32)
    if row_pairs:
        row_order = row ^ ((row_order & 1) * 2 + row_order // 2)
    row_order = row_order * coarse

    solution, field, assembled, maps = load_f, load_f, None, None
    square = 8 * size * size * columns
    for step_index in range(STEPS):
        phase = step_index % DEGREE
        weight = 1.0 / (1.4 - math.cos(math.pi * (2 * phase + 1) / (2 * DEGREE)))
        first = step_index == 0
        if first:
            operands = [load_f] + got + [basis2]
        else:
            operands = [field] + exchange(faces(field)) + [assembled, basis2]
        current, coeffs = call(
            functools.partial(coeffs_kernel, first, face), [(n, F32), ((coarse, columns), F32)], [link], operands
        )
        if first:
            assembled = current

        known = jnp.concatenate([coeffs, map_t]) if first else coeffs
        if row_pairs:
            got_r = swap(known, lambda r, c: (r ^ 2, c))
        y, face_g, face_h = call(
            functools.partial(local_kernel, face),
            [(n, F32), ((face, columns), F32), ((face, columns), F32)],
            [],
            [current, inverse2, perm, back],
            flops=2 * square,
        )
        got_h = swap_odd_row(face_h)
        if row_pairs:
            got_g = swap_even_row(jnp.concatenate([face_g, known, got_r]))
            more = face + known.shape[0]
            pieces, starts = [coeffs, got_r, got_g], ((0,), (0,), (face, more))
            map_starts = ((0,), (coarse,), (face + coarse, more + coarse))
            sources = [map_t, got_r, got_g]
        else:
            got_g = swap_even_row(face_g)
            spans = tuple(range(0, total, coarse))
            pieces, starts = [lax.all_gather(coeffs, "row", axis=0, tiled=True)], (spans,)
            map_starts = starts
            sources = [lax.all_gather(map_t, "row", axis=0, tiled=True)] if first else None
        if first:
            maps = call(
                functools.partial(maps_kernel, coarse, map_starts), [((2 * rows * top, coarse), BF16)], [], sources
            )[0]
        third = call(functools.partial(third_kernel, starts, coarse), [((top, columns), F32)], [], [maps] + pieces)[0]

        if doubling:
            more = swap(third, lambda r, c: (r, c ^ 1))
        y2 = call(
            functools.partial(group_kernel, face, starts, coarse),
            [(n, F32)],
            [link, row_order],
            [y, got_g, got_h, two2] + pieces,
            scratch=[(total, columns)],
        )[0]
        got_f = swap_odd_col(y2[face : 2 * face])
        got_e = swap_even_col(y2[:face])
        if doubling:
            tops, bits = [third, more], 2
            known = jnp.concatenate([third, more])
            while bits < cols:
                more = swap(known, lambda r, c: (r, c ^ bits))
                tops.append(more)
                known = jnp.concatenate([known, more])
                bits *= 2
        else:
            tops = [lax.all_gather(third, "col", axis=0, tiled=True)]
        starts = (0,) * len(tops)
        solution, field = call(
            functools.partial(update_kernel, weight, first, face, starts, top),
            [(n, F32), (n, F32)],
            [link, col_order],
            [y2, got_e, got_f, top2, perm, back, schur2] + ([] if first else [solution]) + tops,
            flops=2 * square,
            scratch=[(width, columns)],
        )
    residual = call(
        functools.partial(residual_kernel, face),
        [(n, F32)],
        [link],
        [field] + exchange(faces(field)) + [assembled, back],
    )[0]
    return (solution[None, None], residual[None, None])


def solution(mesh):
    return jax.shard_map(
        shards,
        mesh=mesh,
        in_specs=(
            P("row", "col", None, None),
            P("row", "col", None, None),
            P("row", "col", None, None),
            P("row", "col", None),
            P("row", "col", None),
            P("row", "col", None, None),
            P("col", "row", None),
            P("col", "row", None),
            P("col", None),
        ),
        out_specs=(P("row", "col", None, None), P("row", "col", None, None)),
        check_vma=False,
    )
```

```python
import functools
import math

import jax
import jax.numpy as jnp
from jax import lax
from jax.experimental import pallas as pl
from jax.experimental.pallas import tpu as pltpu
from jax.sharding import PartitionSpec as P


DEGREE = 2
STEPS = 4
LANES = 128
INTERPRET = False
VMEM_LIMIT = 16 * 2**20
F32 = jnp.float32
BF16 = jnp.bfloat16


def split(x, parts):
    pieces = []
    for _ in range(parts - 1):
        piece = x.astype(BF16)
        pieces.append(piece)
        x = x - piece.astype(F32)
    pieces.append(x.astype(BF16))
    return pieces


def stack_split(x):
    return jnp.concatenate(split(x, 2), axis=0)


def dot(left, right):
    return jnp.dot(left, right, preferred_element_type=F32)


def product_parts(left2, right_parts):
    rows = left2.shape[0] // 2
    n = right_parts[0].shape[1]
    out = dot(left2, jnp.concatenate(right_parts, axis=1))
    out = out[:rows] + out[rows:]
    return out[:, :n] + out[:, n:]


def product(left2, right):
    return product_parts(left2, split(right, 2))


def permuted(onehot, x, parts=2):
    n = x.shape[1]
    out = dot(onehot, jnp.concatenate(split(x, parts), axis=1))
    total = out[:, (parts - 1) * n :]
    for i in reversed(range(parts - 1)):
        total = out[:, i * n : (i + 1) * n] + total
    return total


def call(body, out_shapes, scalars, arrays, flops=0, scratch=()):
    smem = pl.BlockSpec(memory_space=pltpu.SMEM)
    vmem = pl.BlockSpec(memory_space=pltpu.VMEM)
    moved = sum(a.size * a.dtype.itemsize for a in arrays)
    return pl.pallas_call(
        body,
        out_shape=[jax.ShapeDtypeStruct(s, d) for s, d in out_shapes],
        in_specs=[smem] * len(scalars) + [vmem] * len(arrays),
        out_specs=[vmem] * len(out_shapes),
        scratch_shapes=[pltpu.VMEM(shape, F32) for shape in scratch],
        compiler_params=pltpu.CompilerParams(vmem_limit_bytes=VMEM_LIMIT),
        cost_estimate=pl.CostEstimate(flops=flops, bytes_accessed=moved, transcendentals=0),
        interpret=INTERPRET,
    )(*scalars, *arrays)


def pack(ref, start, x):
    rows, width = x.shape
    for i in range(0, width, LANES):
        w = min(LANES, width - i)
        ref[start : start + rows, :w] = x[:, i : i + w]
        start += rows
    return start


def unpack(ref, start, rows, width):
    parts = []
    for i in range(0, width, LANES):
        parts.append(ref[start : start + rows, : min(LANES, width - i)])
        start += rows
    return jnp.concatenate(parts, axis=1) if len(parts) > 1 else parts[0]


def blocks(width):
    return -(-width // LANES)


def pack_halves(ref, start, x):
    half = x.shape[0] // 2
    ref[start : start + half, : x.shape[1]] = x[:half]
    ref[start : start + half, LANES // 2 : LANES // 2 + x.shape[1]] = x[half:]


def unpack_halves(ref, start, rows, width):
    x = ref[start : start + rows // 2, :]
    return jnp.concatenate([x[:, :width], x[:, LANES // 2 : LANES // 2 + width]], axis=0)


def transposed(x, pad_ref):
    rows, width = x.shape
    pad_ref[...] = jnp.zeros_like(pad_ref)
    pad_ref[:rows, :width] = x
    return pad_ref[...].T[:width, :rows]


def index_kernel(face, columns, place_ref, index_ref, load_ref, perm_ref, back_ref, load_out):
    size = perm_ref.shape[0]
    raw = index_ref[...].astype(F32)
    west, east, south, north = [raw[:, k * face : (k + 1) * face] for k in range(4)]
    even_row, even_col = place_ref[0] % 2 == 0, place_ref[1] % 2 == 0
    index = jnp.concatenate(
        [
            jnp.where(even_col, east, west),
            jnp.where(even_col, west, east),
            jnp.where(even_row, north, south),
            jnp.where(even_row, south, north),
        ],
        axis=1,
    )
    tall = jnp.broadcast_to(index, (LANES, size)).T
    lane = lax.broadcasted_iota(jnp.int32, (size, LANES), 1).astype(F32)
    for i in range(0, size, LANES):
        perm_ref[:, i : i + LANES] = jnp.where(tall == lane + float(i), 1.0, 0.0).astype(BF16)
    down = lax.broadcasted_iota(jnp.int32, (size, size), 0).astype(F32)
    back_ref[...] = jnp.where(index == down, 1.0, 0.0).astype(BF16)
    load_out[...] = permuted(perm_ref[...], load_ref[:, :columns])


def start_kernel(
    face,
    shapes,
    perm_ref,
    load_ref,
    basis_ref,
    small_in_ref,
    basis_out,
    coarse_out,
    basis2_ref,
    map_t_ref,
    inverse_out,
    top_out,
    e_ref,
    f_ref,
    g_ref,
    h_ref,
    tall_ref,
    small_ref,
):
    coarse, total, top, _ = shapes
    columns = load_ref.shape[1]
    level = small_in_ref[:, : total + top]
    inverse, mapped, tops = level[:, :total], level[:, total:], small_in_ref[:, blocks(total + top) * LANES :]
    basis = permuted(perm_ref[...], basis_ref[:, columns : columns + coarse])
    basis_out[...] = basis
    product_map = product(stack_split(basis), mapped)
    coarse_out[...] = product_map
    inverse_out[...] = inverse
    top_out[...] = tops
    for k, ref in enumerate((e_ref, f_ref, g_ref, h_ref)):
        rows = slice(k * face, (k + 1) * face)
        ref[:face] = load_ref[rows]
        ref[face:] = jnp.zeros((ref.shape[0] - face, ref.shape[1]), F32)
        pack_halves(ref, face, product_map[rows] if k < 2 else basis[rows])
        pack(ref, face + face // 2, tops if k < 2 else level)
    basis2_ref[...] = stack_split(transposed(basis, tall_ref))
    map_t_ref[...] = jnp.zeros_like(map_t_ref)
    map_t_ref[:, :coarse] = transposed(mapped, small_ref)


def split_kernel(x_ref, o_ref):
    o_ref[...] = stack_split(x_ref[...])


def level_kernel(
    face, link_ref, basis_ref, inverse_ref, coarse_ref, top_ref, e_ref, f_ref, g_ref, h_ref, two_ref, top_out_ref
):
    coarse, total = inverse_ref.shape
    top, width = top_ref.shape
    start = face + face // 2
    link = [link_ref[i].astype(F32) for i in range(4)]
    two = product(stack_split(basis_ref[...]), inverse_ref[...])
    third = coarse_ref[...]
    twos, thirds = [two[: 2 * face]], [third[: 2 * face]]
    for k, ref in ((2, g_ref), (3, h_ref)):
        rows = slice(k * face, (k + 1) * face)
        basis = stack_split(unpack_halves(ref, face, face, coarse) * link[k])
        level = product(basis, unpack(ref, start, coarse, total + top))
        twos.append(two[rows] + level[:, :total])
        thirds.append(third[rows] + level[:, total:])
    two_ref[...] = stack_split(jnp.concatenate(twos, axis=0))
    out = product(stack_split(jnp.concatenate(thirds, axis=0)), top_ref[...])
    outs = []
    for k, ref in ((0, e_ref), (1, f_ref)):
        rows = slice(k * face, (k + 1) * face)
        near = stack_split(unpack_halves(ref, face, face, top) * link[k])
        outs.append(out[rows] + product(near, unpack(ref, start, top, width)))
    top_out_ref[...] = stack_split(jnp.concatenate(outs + [out[2 * face :]], axis=0))


def received(face, link_ref, refs):
    return jnp.concatenate([r[:face] * link_ref[i].astype(F32) for i, r in enumerate(refs)], axis=0)


def coeffs_kernel(first, face, link_ref, f_ref, r0, r1, r2, r3, *refs):
    field = f_ref[...] + received(face, link_ref, (r0, r1, r2, r3))
    if first:
        basis_ref, current_ref, c_ref = refs
        current = field
    else:
        asm_ref, basis_ref, current_ref, c_ref = refs
        current = asm_ref[...] - field
    current_ref[...] = current
    c_ref[...] = product(basis_ref[...], current)


def local_kernel(face, current_ref, inverse_ref, perm_ref, back_ref, y_ref, g_ref, h_ref):
    n = current_ref.shape[1]
    moved = dot(back_ref[...], jnp.concatenate(split(current_ref[...], 2), axis=1)).astype(BF16)
    y = permuted(perm_ref[...], product_parts(inverse_ref[...], [moved[:, :n], moved[:, n:]]))
    y_ref[...] = y
    g_ref[...] = y[2 * face : 3 * face]
    h_ref[...] = y[3 * face :]


def maps_kernel(coarse, starts, *refs):
    out_ref = refs[-1]
    slot = 0
    for ref, spans in zip(refs, starts):
        for start in spans:
            part = stack_split(ref[start : start + coarse, :coarse])
            out_ref[slot * part.shape[0] : (slot + 1) * part.shape[0]] = part
            slot += 1


def third_kernel(starts, coarse, maps_ref, *refs):
    third, slot = None, 0
    rows = maps_ref.shape[0] // sum(len(spans) for spans in starts)
    for ref, spans in zip(refs, starts):
        for start in spans:
            part = product(maps_ref[slot * rows : (slot + 1) * rows], ref[start : start + coarse])
            third = part if third is None else third + part
            slot += 1
    refs[-1][...] = third


def group_kernel(face, starts, coarse, link_ref, order_ref, y_ref, g_ref, h_ref, two_ref, *refs):
    y2_ref, stack_ref = refs[len(starts) :]
    slot = 0
    for ref, spans in zip(refs, starts):
        for start in spans:
            offset = pl.multiple_of(order_ref[slot], 8)
            stack_ref[pl.ds(offset, coarse)] = ref[start : start + coarse]
            slot += 1
    y = y_ref[...] + product(two_ref[...], stack_ref[...])
    y2_ref[: 2 * face] = y[: 2 * face]
    y2_ref[2 * face : 3 * face] = y[2 * face : 3 * face] + g_ref[:face] * link_ref[2].astype(F32)
    y2_ref[3 * face :] = y[3 * face :] + h_ref[:face] * link_ref[3].astype(F32)


def update_kernel(
    weight, first, face, starts, top, link_ref, order_ref, y2_ref, e_ref, f_ref, top_ref, perm_ref, back_ref, schur_ref, *refs
):
    if not first:
        old_ref, refs = refs[0], refs[1:]
    x_ref, out_ref, stack_ref = refs[len(starts) :]
    slot = 0
    for ref, first_row in zip(refs, starts):
        for start in range(first_row, ref.shape[0], top):
            stack_ref[pl.ds(pl.multiple_of(order_ref[slot], 8), top)] = ref[start : start + top]
            slot += 1
    y2 = y2_ref[...] + product(top_ref[...], stack_ref[...])
    update = jnp.concatenate(
        [
            y2[:face] + e_ref[:face] * link_ref[0].astype(F32),
            y2[face : 2 * face] + f_ref[:face] * link_ref[1].astype(F32),
            y2[2 * face :],
        ],
        axis=0,
    )
    x = weight * permuted(back_ref[...], update)
    if not first:
        x = old_ref[...] + x
    x_ref[...] = x
    out_ref[...] = permuted(perm_ref[...], product(schur_ref[...], x))


def residual_kernel(face, link_ref, f_ref, r0, r1, r2, r3, asm_ref, back_ref, out_ref):
    current = asm_ref[...] - (f_ref[...] + received(face, link_ref, (r0, r1, r2, r3)))
    out_ref[...] = permuted(back_ref[...], current)


def swap_pairs(rows, cols, partner):
    pairs = []
    for r in range(rows):
        for c in range(cols):
            a, b = partner(r, c)
            if not (0 <= a < rows and 0 <= b < cols):
                a, b = (r, c ^ 1) if not 0 <= a < rows else (r ^ 1, c)
            if a < rows and b < cols:
                pairs.append((r * cols + c, a * cols + b))
    return pairs


def odd_neighbour(i):
    return i + 1 if i % 2 else i - 1


def shards(
    load,
    schur,
    local_inverse,
    iface_index,
    face_link,
    coarse_basis,
    coarse_inverse,
    coarse_map,
    top_inverse,
):
    loads, basis = load[0, 0], coarse_basis[0, 0]
    inverse_rows, map_block = coarse_inverse[0], coarse_map[0]
    size, columns = loads.shape
    face = size // 4
    coarse, top = basis.shape[1], map_block.shape[1]
    rows, cols = lax.axis_size("row"), lax.axis_size("col")
    row, col = lax.axis_index("row"), lax.axis_index("col")
    total, width = inverse_rows.shape[1], top_inverse.shape[1]

    place = jnp.stack([row, col])
    side = jnp.arange(4, dtype=jnp.int32)
    parity = jnp.where(side < 2, col, row) & 1
    facing = jnp.where(side < 2, 0, 2) + ((side & 1) ^ parity ^ 1)
    link = jnp.sum(jnp.where(facing[:, None] == side[None, :], face_link[0, 0][None, :], 0), axis=1)

    def swap(x, partner):
        return lax.ppermute(x, ("row", "col"), swap_pairs(rows, cols, partner))

    def swap_even_col(x):
        return swap(x, lambda r, c: (r, c ^ 1))

    def swap_odd_col(x):
        return swap(x, lambda r, c: (r, odd_neighbour(c)))

    def swap_even_row(x):
        return swap(x, lambda r, c: (r ^ 1, c))

    def swap_odd_row(x):
        return swap(x, lambda r, c: (odd_neighbour(r), c))

    def exchange(parts):
        got_f = swap_odd_col(parts[1])
        got_g = swap_even_row(parts[2])
        got_h = swap_odd_row(parts[3])
        got_e = swap_even_col(parts[0])
        return [got_e, got_f, got_g, got_h]

    row_pairs = rows == 4

    def faces(x):
        return [x[i * face : (i + 1) * face] for i in range(4)]

    n = (size, columns)
    common = face + face // 2
    payloads = [common + blocks(width) * top] * 2 + [common + blocks(total + top) * coarse] * 2
    wide = jnp.concatenate([loads, basis], axis=1)
    gap = jnp.zeros((coarse, blocks(total + top) * LANES - total - top), F32)
    small = jnp.concatenate([inverse_rows, map_block, gap, top_inverse], axis=1)
    perm, back, load_f = call(
        functools.partial(index_kernel, face, columns),
        [((size, size), BF16), ((size, size), BF16), (n, F32)],
        [place],
        [iface_index[0], wide],
        flops=4 * size**2 * columns,
    )
    basis_f, coarse_f, basis2, map_t, inverse_rows, top_inverse, *sent = call(
        functools.partial(start_kernel, face, (coarse, total, top, width)),
        [((size, coarse), F32), ((size, top), F32), ((2 * coarse, size), BF16), ((top, columns), F32)]
        + [(inverse_rows.shape, F32), (top_inverse.shape, F32)]
        + [((p, columns), F32) for p in payloads],
        [],
        [perm, load_f, wide, small],
        flops=4 * size**2 * columns,
        scratch=[(size, LANES), (LANES, LANES)],
    )
    schur2 = call(split_kernel, [((2 * size, size), BF16)], [], [schur[0, 0]])[0]
    inverse2 = call(split_kernel, [((2 * size, size), BF16)], [], [local_inverse[0, 0]])[0]

    got = exchange(sent)
    two2, top2 = call(
        functools.partial(level_kernel, face),
        [((2 * size, total), BF16), ((2 * size, width), BF16)],
        [link],
        [basis_f, inverse_rows, coarse_f, top_inverse] + got,
    )

    doubling = cols & (cols - 1) == 0
    col_order = jnp.arange(cols, dtype=jnp.int32)
    if doubling:
        rest = sum((col_order >> i & 1) for i in range(1, cols.bit_length() - 1))
        col_order = col ^ col_order ^ (rest & 1)
    col_order = col_order * top
    row_order = jnp.arange(rows, dtype=jnp.int32)
    if row_pairs:
        row_order = row ^ ((row_order & 1) * 2 + row_order // 2)
    row_order = row_order * coarse

    solution, field, assembled, maps = load_f, load_f, None, None
    square = 8 * size * size * columns
    for step_index in range(STEPS):
        phase = step_index % DEGREE
        weight = 1.0 / (1.4 - math.cos(math.pi * (2 * phase + 1) / (2 * DEGREE)))
        first = step_index == 0
        if first:
            operands = [load_f] + got + [basis2]
        else:
            operands = [field] + exchange(faces(field)) + [assembled, basis2]
        current, coeffs = call(
            functools.partial(coeffs_kernel, first, face), [(n, F32), ((coarse, columns), F32)], [link], operands
        )
        if first:
            assembled = current

        known = jnp.concatenate([coeffs, map_t]) if first else coeffs
        if row_pairs:
            got_r = swap(known, lambda r, c: (r ^ 2, c))
        y, face_g, face_h = call(
            functools.partial(local_kernel, face),
            [(n, F32), ((face, columns), F32), ((face, columns), F32)],
            [],
            [current, inverse2, perm, back],
            flops=2 * square,
        )
        got_h = swap_odd_row(face_h)
        if row_pairs:
            got_g = swap_even_row(jnp.concatenate([face_g, known, got_r]))
            more = face + known.shape[0]
            pieces, starts = [coeffs, got_r, got_g], ((0,), (0,), (face, more))
            map_starts = ((0,), (coarse,), (face + coarse, more + coarse))
            sources = [map_t, got_r, got_g]
        else:
            got_g = swap_even_row(face_g)
            spans = tuple(range(0, total, coarse))
            pieces, starts = [lax.all_gather(coeffs, "row", axis=0, tiled=True)], (spans,)
            map_starts = starts
            sources = [lax.all_gather(map_t, "row", axis=0, tiled=True)] if first else None
        if first:
            maps = call(
                functools.partial(maps_kernel, coarse, map_starts), [((2 * rows * top, coarse), BF16)], [], sources
            )[0]
        third = call(functools.partial(third_kernel, starts, coarse), [((top, columns), F32)], [], [maps] + pieces)[0]

        if doubling:
            more = swap(third, lambda r, c: (r, c ^ 1))
        y2 = call(
            functools.partial(group_kernel, face, starts, coarse),
            [(n, F32)],
            [link, row_order],
            [y, got_g, got_h, two2] + pieces,
            scratch=[(total, columns)],
        )[0]
        got_f = swap_odd_col(y2[face : 2 * face])
        got_e = swap_even_col(y2[:face])
        if doubling:
            tops, bits = [third, more], 2
            known = jnp.concatenate([third, more])
            while bits < cols:
                more = swap(known, lambda r, c: (r, c ^ bits ^ 1))
                tops.append(more)
                known = jnp.concatenate([known, more])
                bits *= 2
        else:
            tops = [lax.all_gather(third, "col", axis=0, tiled=True)]
        starts = (0,) * len(tops)
        solution, field = call(
            functools.partial(update_kernel, weight, first, face, starts, top),
            [(n, F32), (n, F32)],
            [link, col_order],
            [y2, got_e, got_f, top2, perm, back, schur2] + ([] if first else [solution]) + tops,
            flops=2 * square,
            scratch=[(width, columns)],
        )
    residual = call(
        functools.partial(residual_kernel, face),
        [(n, F32)],
        [link],
        [field] + exchange(faces(field)) + [assembled, back],
    )[0]
    return (solution[None, None], residual[None, None])


def solution(mesh):
    return jax.shard_map(
        shards,
        mesh=mesh,
        in_specs=(
            P("row", "col", None, None),
            P("row", "col", None, None),
            P("row", "col", None, None),
            P("row", "col", None),
            P("row", "col", None),
            P("row", "col", None, None),
            P("col", "row", None),
            P("col", "row", None),
            P("col", None),
        ),
        out_specs=(P("row", "col", None, None), P("row", "col", None, None)),
        check_vma=False,
    )
```

```python
import functools
import math

import jax
import jax.numpy as jnp
from jax import lax
from jax.experimental import pallas as pl
from jax.experimental.pallas import tpu as pltpu
from jax.sharding import PartitionSpec as P


DEGREE = 2
STEPS = 4
LANES = 128
INTERPRET = False
VMEM_LIMIT = 16 * 2**20
F32 = jnp.float32
BF16 = jnp.bfloat16


def split(x, parts):
    pieces = []
    for _ in range(parts - 1):
        piece = x.astype(BF16)
        pieces.append(piece)
        x = x - piece.astype(F32)
    pieces.append(x.astype(BF16))
    return pieces


def stack_split(x):
    return jnp.concatenate(split(x, 2), axis=0)


def dot(left, right):
    return jnp.dot(left, right, preferred_element_type=F32)


def product_parts(left2, right_parts):
    rows = left2.shape[0] // 2
    n = right_parts[0].shape[1]
    out = dot(left2, jnp.concatenate(right_parts, axis=1))
    out = out[:rows] + out[rows:]
    return out[:, :n] + out[:, n:]


def product(left2, right):
    return product_parts(left2, split(right, 2))


def permuted(onehot, x, parts=2):
    n = x.shape[1]
    out = dot(onehot, jnp.concatenate(split(x, parts), axis=1))
    total = out[:, (parts - 1) * n :]
    for i in reversed(range(parts - 1)):
        total = out[:, i * n : (i + 1) * n] + total
    return total


def call(body, out_shapes, scalars, arrays, flops=0, scratch=()):
    smem = pl.BlockSpec(memory_space=pltpu.SMEM)
    vmem = pl.BlockSpec(memory_space=pltpu.VMEM)
    moved = sum(a.size * a.dtype.itemsize for a in arrays)
    return pl.pallas_call(
        body,
        out_shape=[jax.ShapeDtypeStruct(s, d) for s, d in out_shapes],
        in_specs=[smem] * len(scalars) + [vmem] * len(arrays),
        out_specs=[vmem] * len(out_shapes),
        scratch_shapes=[pltpu.VMEM(shape, F32) for shape in scratch],
        compiler_params=pltpu.CompilerParams(vmem_limit_bytes=VMEM_LIMIT),
        cost_estimate=pl.CostEstimate(flops=flops, bytes_accessed=moved, transcendentals=0),
        interpret=INTERPRET,
    )(*scalars, *arrays)


def pack(ref, start, x):
    rows, width = x.shape
    for i in range(0, width, LANES):
        w = min(LANES, width - i)
        ref[start : start + rows, :w] = x[:, i : i + w]
        start += rows
    return start


def unpack(ref, start, rows, width):
    parts = []
    for i in range(0, width, LANES):
        parts.append(ref[start : start + rows, : min(LANES, width - i)])
        start += rows
    return jnp.concatenate(parts, axis=1) if len(parts) > 1 else parts[0]


def blocks(width):
    return -(-width // LANES)


def pack_halves(ref, start, x):
    half = x.shape[0] // 2
    ref[start : start + half, : x.shape[1]] = x[:half]
    ref[start : start + half, LANES // 2 : LANES // 2 + x.shape[1]] = x[half:]


def unpack_halves(ref, start, rows, width):
    x = ref[start : start + rows // 2, :]
    return jnp.concatenate([x[:, :width], x[:, LANES // 2 : LANES // 2 + width]], axis=0)


def transposed(x, pad_ref):
    rows, width = x.shape
    pad_ref[...] = jnp.zeros_like(pad_ref)
    pad_ref[:rows, :width] = x
    return pad_ref[...].T[:width, :rows]


def index_kernel(face, columns, place_ref, index_ref, load_ref, perm_ref, back_ref, load_out):
    size = perm_ref.shape[0]
    raw = index_ref[...].astype(F32)
    west, east, south, north = [raw[:, k * face : (k + 1) * face] for k in range(4)]
    even_row, even_col = place_ref[0] % 2 == 0, place_ref[1] % 2 == 0
    index = jnp.concatenate(
        [
            jnp.where(even_col, east, west),
            jnp.where(even_col, west, east),
            jnp.where(even_row, north, south),
            jnp.where(even_row, south, north),
        ],
        axis=1,
    )
    tall = jnp.broadcast_to(index, (LANES, size)).T
    lane = lax.broadcasted_iota(jnp.int32, (size, LANES), 1).astype(F32)
    for i in range(0, size, LANES):
        perm_ref[:, i : i + LANES] = jnp.where(tall == lane + float(i), 1.0, 0.0).astype(BF16)
    down = lax.broadcasted_iota(jnp.int32, (size, size), 0).astype(F32)
    back_ref[...] = jnp.where(index == down, 1.0, 0.0).astype(BF16)
    load_out[...] = permuted(perm_ref[...], load_ref[:, :columns])


def start_kernel(
    face,
    shapes,
    perm_ref,
    load_ref,
    basis_ref,
    small_in_ref,
    basis_out,
    coarse_out,
    basis2_ref,
    map_t_ref,
    inverse_out,
    top_out,
    e_ref,
    f_ref,
    g_ref,
    h_ref,
    tall_ref,
    small_ref,
):
    coarse, total, top, _ = shapes
    columns = load_ref.shape[1]
    level = small_in_ref[:, : total + top]
    inverse, mapped, tops = level[:, :total], level[:, total:], small_in_ref[:, blocks(total + top) * LANES :]
    basis = permuted(perm_ref[...], basis_ref[:, columns : columns + coarse])
    basis_out[...] = basis
    product_map = product(stack_split(basis), mapped)
    coarse_out[...] = product_map
    inverse_out[...] = inverse
    top_out[...] = tops
    for k, ref in enumerate((e_ref, f_ref, g_ref, h_ref)):
        rows = slice(k * face, (k + 1) * face)
        ref[:face] = load_ref[rows]
        ref[face:] = jnp.zeros((ref.shape[0] - face, ref.shape[1]), F32)
        pack_halves(ref, face, product_map[rows] if k < 2 else basis[rows])
        pack(ref, face + face // 2, tops if k < 2 else level)
    basis2_ref[...] = stack_split(transposed(basis, tall_ref))
    map_t_ref[...] = jnp.zeros_like(map_t_ref)
    map_t_ref[:, :coarse] = transposed(mapped, small_ref)


def fold_kernel(perm_ref, x_ref, *refs):
    rows = x_ref.shape[0]
    for i, part in enumerate(split(x_ref[...], 2)):
        part = dot(perm_ref[...], part).astype(BF16)
        if len(refs) > 1:
            part = dot(part, refs[0][...]).astype(BF16)
        refs[-1][i * rows : (i + 1) * rows] = part


def restore_kernel(x_ref, back_ref, out_ref):
    out_ref[...] = permuted(back_ref[...], x_ref[...], 3)


def level_kernel(
    face, link_ref, basis_ref, inverse_ref, coarse_ref, top_ref, e_ref, f_ref, g_ref, h_ref, two_ref, top_out_ref
):
    coarse, total = inverse_ref.shape
    top, width = top_ref.shape
    start = face + face // 2
    link = [link_ref[i].astype(F32) for i in range(4)]
    two = product(stack_split(basis_ref[...]), inverse_ref[...])
    third = coarse_ref[...]
    twos, thirds = [two[: 2 * face]], [third[: 2 * face]]
    for k, ref in ((2, g_ref), (3, h_ref)):
        rows = slice(k * face, (k + 1) * face)
        basis = stack_split(unpack_halves(ref, face, face, coarse) * link[k])
        level = product(basis, unpack(ref, start, coarse, total + top))
        twos.append(two[rows] + level[:, :total])
        thirds.append(third[rows] + level[:, total:])
    two_ref[...] = stack_split(jnp.concatenate(twos, axis=0))
    out = product(stack_split(jnp.concatenate(thirds, axis=0)), top_ref[...])
    outs = []
    for k, ref in ((0, e_ref), (1, f_ref)):
        rows = slice(k * face, (k + 1) * face)
        near = stack_split(unpack_halves(ref, face, face, top) * link[k])
        outs.append(out[rows] + product(near, unpack(ref, start, top, width)))
    top_out_ref[...] = stack_split(jnp.concatenate(outs + [out[2 * face :]], axis=0))


def received(face, link_ref, refs):
    return jnp.concatenate([r[:face] * link_ref[i].astype(F32) for i, r in enumerate(refs)], axis=0)


def coeffs_kernel(first, face, link_ref, f_ref, r0, r1, r2, r3, *refs):
    field = f_ref[...] + received(face, link_ref, (r0, r1, r2, r3))
    if first:
        basis_ref, current_ref, c_ref = refs
        current = field
    else:
        asm_ref, basis_ref, current_ref, c_ref = refs
        current = asm_ref[...] - field
    current_ref[...] = current
    c_ref[...] = product(basis_ref[...], current)


def local_kernel(face, current_ref, inverse_ref, back_ref, y_ref, g_ref, h_ref):
    n = current_ref.shape[1]
    moved = dot(back_ref[...], jnp.concatenate(split(current_ref[...], 2), axis=1)).astype(BF16)
    y = product_parts(inverse_ref[...], [moved[:, :n], moved[:, n:]])
    y_ref[...] = y
    g_ref[...] = y[2 * face : 3 * face]
    h_ref[...] = y[3 * face :]


def maps_kernel(coarse, starts, *refs):
    out_ref = refs[-1]
    slot = 0
    for ref, spans in zip(refs, starts):
        for start in spans:
            part = stack_split(ref[start : start + coarse, :coarse])
            out_ref[slot * part.shape[0] : (slot + 1) * part.shape[0]] = part
            slot += 1


def third_kernel(starts, coarse, maps_ref, *refs):
    third, slot = None, 0
    rows = maps_ref.shape[0] // sum(len(spans) for spans in starts)
    for ref, spans in zip(refs, starts):
        for start in spans:
            part = product(maps_ref[slot * rows : (slot + 1) * rows], ref[start : start + coarse])
            third = part if third is None else third + part
            slot += 1
    refs[-1][...] = third


def group_kernel(starts, coarse, order_ref, y_ref, two_ref, *refs):
    y2_ref, stack_ref = refs[len(starts) :]
    slot = 0
    for ref, spans in zip(refs, starts):
        for start in spans:
            offset = pl.multiple_of(order_ref[slot], 8)
            stack_ref[pl.ds(offset, coarse)] = ref[start : start + coarse]
            slot += 1
    y2_ref[...] = y_ref[...] + product(two_ref[...], stack_ref[...])


def update_kernel(
    weight, first, face, top, link_ref, order_ref, y2_ref, r0, r1, r2, r3, top_ref, schur_ref, *refs
):
    if not first:
        old_ref, refs = refs[0], refs[1:]
    x_ref, out_ref, stack_ref = refs[-3:]
    slot = 0
    for ref in refs[:-3]:
        for start in range(0, ref.shape[0], top):
            stack_ref[pl.ds(pl.multiple_of(order_ref[slot], 8), top)] = ref[start : start + top]
            slot += 1
    update = y2_ref[...] + received(face, link_ref, (r0, r1, r2, r3)) + product(top_ref[...], stack_ref[...])
    x = weight * update
    if not first:
        x = old_ref[...] + x
    x_ref[...] = x
    out_ref[...] = product(schur_ref[...], x)


def residual_kernel(face, link_ref, f_ref, r0, r1, r2, r3, asm_ref, back_ref, out_ref):
    current = asm_ref[...] - (f_ref[...] + received(face, link_ref, (r0, r1, r2, r3)))
    out_ref[...] = permuted(back_ref[...], current)


def swap_pairs(rows, cols, partner):
    pairs = []
    for r in range(rows):
        for c in range(cols):
            a, b = partner(r, c)
            if not (0 <= a < rows and 0 <= b < cols):
                a, b = (r, c ^ 1) if not 0 <= a < rows else (r ^ 1, c)
            if a < rows and b < cols:
                pairs.append((r * cols + c, a * cols + b))
    return pairs


def odd_neighbour(i):
    return i + 1 if i % 2 else i - 1


def shards(
    load,
    schur,
    local_inverse,
    iface_index,
    face_link,
    coarse_basis,
    coarse_inverse,
    coarse_map,
    top_inverse,
):
    loads, basis = load[0, 0], coarse_basis[0, 0]
    inverse_rows, map_block = coarse_inverse[0], coarse_map[0]
    size, columns = loads.shape
    face = size // 4
    coarse, top = basis.shape[1], map_block.shape[1]
    rows, cols = lax.axis_size("row"), lax.axis_size("col")
    row, col = lax.axis_index("row"), lax.axis_index("col")
    total, width = inverse_rows.shape[1], top_inverse.shape[1]

    place = jnp.stack([row, col])
    side = jnp.arange(4, dtype=jnp.int32)
    parity = jnp.where(side < 2, col, row) & 1
    facing = jnp.where(side < 2, 0, 2) + ((side & 1) ^ parity ^ 1)
    link = jnp.sum(jnp.where(facing[:, None] == side[None, :], face_link[0, 0][None, :], 0), axis=1)

    def swap(x, partner):
        return lax.ppermute(x, ("row", "col"), swap_pairs(rows, cols, partner))

    def swap_even_col(x):
        return swap(x, lambda r, c: (r, c ^ 1))

    def swap_odd_col(x):
        return swap(x, lambda r, c: (r, odd_neighbour(c)))

    def swap_even_row(x):
        return swap(x, lambda r, c: (r ^ 1, c))

    def swap_odd_row(x):
        return swap(x, lambda r, c: (odd_neighbour(r), c))

    def exchange(parts):
        got_f = swap_odd_col(parts[1])
        got_g = swap_even_row(parts[2])
        got_h = swap_odd_row(parts[3])
        got_e = swap_even_col(parts[0])
        return [got_e, got_f, got_g, got_h]

    row_pairs = rows == 4

    def faces(x):
        return [x[i * face : (i + 1) * face] for i in range(4)]

    n = (size, columns)
    common = face + face // 2
    payloads = [common + blocks(width) * top] * 2 + [common + blocks(total + top) * coarse] * 2
    wide = jnp.concatenate([loads, basis], axis=1)
    gap = jnp.zeros((coarse, blocks(total + top) * LANES - total - top), F32)
    small = jnp.concatenate([inverse_rows, map_block, gap, top_inverse], axis=1)
    perm, back, load_f = call(
        functools.partial(index_kernel, face, columns),
        [((size, size), BF16), ((size, size), BF16), (n, F32)],
        [place],
        [iface_index[0], wide],
        flops=4 * size**2 * columns,
    )
    basis_f, coarse_f, basis2, map_t, inverse_rows, top_inverse, *sent = call(
        functools.partial(start_kernel, face, (coarse, total, top, width)),
        [((size, coarse), F32), ((size, top), F32), ((2 * coarse, size), BF16), ((top, columns), F32)]
        + [(inverse_rows.shape, F32), (top_inverse.shape, F32)]
        + [((p, columns), F32) for p in payloads],
        [],
        [perm, load_f, wide, small],
        flops=4 * size**2 * columns,
        scratch=[(size, LANES), (LANES, LANES)],
    )

    def folded(x, *more):
        return call(fold_kernel, [((2 * size, size), BF16)], [], [perm, x, *more], flops=4 * size**3)[0]

    inverse2 = folded(local_inverse[0, 0])
    schur2 = folded(schur[0, 0], back)

    got = exchange(sent)
    two2, top2 = call(
        functools.partial(level_kernel, face),
        [((2 * size, total), BF16), ((2 * size, width), BF16)],
        [link],
        [basis_f, inverse_rows, coarse_f, top_inverse] + got,
    )

    doubling = cols & (cols - 1) == 0
    col_order = jnp.arange(cols, dtype=jnp.int32)
    if doubling:
        rest = sum((col_order >> i & 1) for i in range(1, cols.bit_length() - 1))
        col_order = col ^ col_order ^ (rest & 1)
    col_order = col_order * top
    row_order = jnp.arange(rows, dtype=jnp.int32)
    if row_pairs:
        row_order = row ^ ((row_order & 1) * 2 + row_order // 2)
    row_order = row_order * coarse

    solution, field, assembled, maps = load_f, load_f, None, None
    square = 8 * size * size * columns
    for step_index in range(STEPS):
        phase = step_index % DEGREE
        weight = 1.0 / (1.4 - math.cos(math.pi * (2 * phase + 1) / (2 * DEGREE)))
        first = step_index == 0
        if first:
            operands = [load_f] + got + [basis2]
        else:
            operands = [field] + exchange(faces(field)) + [assembled, basis2]
        current, coeffs = call(
            functools.partial(coeffs_kernel, first, face), [(n, F32), ((coarse, columns), F32)], [link], operands
        )
        if first:
            assembled = current

        known = jnp.concatenate([coeffs, map_t]) if first else coeffs
        if row_pairs:
            got_r = swap(known, lambda r, c: (r ^ 2, c))
        y, face_g, face_h = call(
            functools.partial(local_kernel, face),
            [(n, F32), ((face, columns), F32), ((face, columns), F32)],
            [],
            [current, inverse2, back],
            flops=2 * square,
        )
        if row_pairs:
            got = swap(jnp.concatenate([known, got_r]), lambda r, c: (r ^ 1, c))
            more = known.shape[0]
            pieces, starts = [coeffs, got_r, got], ((0,), (0,), (0, more))
            map_starts, sources = ((0,), (coarse,), (coarse, more + coarse)), [map_t, got_r, got]
        else:
            pieces = [lax.all_gather(coeffs, "row", axis=0, tiled=True)]
            starts = map_starts = (tuple(range(0, total, coarse)),)
            sources = [lax.all_gather(map_t, "row", axis=0, tiled=True)] if first else None
        got_g = swap_even_row(face_g)
        got_h = swap_odd_row(face_h)
        if first:
            maps = call(
                functools.partial(maps_kernel, coarse, map_starts), [((2 * rows * top, coarse), BF16)], [], sources
            )[0]
        third = call(functools.partial(third_kernel, starts, coarse), [((top, columns), F32)], [], [maps] + pieces)[0]

        if doubling:
            more = swap(third, lambda r, c: (r, c ^ 1))
        y2 = call(
            functools.partial(group_kernel, starts, coarse),
            [(n, F32)],
            [row_order],
            [y, two2] + pieces,
            scratch=[(total, columns)],
        )[0]
        got_f = swap_odd_col(y2[face : 2 * face])
        got_e = swap_even_col(y2[:face])
        if doubling:
            tops, bits = [third, more], 2
            known = jnp.concatenate([third, more])
            while bits < cols:
                more = swap(known, lambda r, c: (r, c ^ bits ^ 1))
                tops.append(more)
                known = jnp.concatenate([known, more])
                bits *= 2
        else:
            tops = [lax.all_gather(third, "col", axis=0, tiled=True)]
        solution, field = call(
            functools.partial(update_kernel, weight, first, face, top),
            [(n, F32), (n, F32)],
            [link, col_order],
            [y2, got_e, got_f, got_g, got_h, top2, schur2] + ([] if first else [solution]) + tops,
            flops=2 * square,
            scratch=[(width, columns)],
        )
    solution = call(restore_kernel, [(n, F32)], [], [solution, back], flops=square)[0]
    residual = call(
        functools.partial(residual_kernel, face),
        [(n, F32)],
        [link],
        [field] + exchange(faces(field)) + [assembled, back],
    )[0]
    return (solution[None, None], residual[None, None])


def solution(mesh):
    return jax.shard_map(
        shards,
        mesh=mesh,
        in_specs=(
            P("row", "col", None, None),
            P("row", "col", None, None),
            P("row", "col", None, None),
            P("row", "col", None),
            P("row", "col", None),
            P("row", "col", None, None),
            P("col", "row", None),
            P("col", "row", None),
            P("col", None),
        ),
        out_specs=(P("row", "col", None, None), P("row", "col", None, None)),
        check_vma=False,
    )
```

```python
import functools
import math

import jax
import jax.numpy as jnp
from jax import lax
from jax.experimental import pallas as pl
from jax.experimental.pallas import tpu as pltpu
from jax.sharding import PartitionSpec as P


DEGREE = 2
STEPS = 4
LANES = 128
INTERPRET = False
VMEM_LIMIT = 16 * 2**20
F32 = jnp.float32
BF16 = jnp.bfloat16


def split(x, parts):
    pieces = []
    for _ in range(parts - 1):
        piece = x.astype(BF16)
        pieces.append(piece)
        x = x - piece.astype(F32)
    pieces.append(x.astype(BF16))
    return pieces


def stack_split(x):
    return jnp.concatenate(split(x, 2), axis=0)


def dot(left, right):
    return jnp.dot(left, right, preferred_element_type=F32)


def product_parts(left2, right_parts):
    rows = left2.shape[0] // 2
    n = right_parts[0].shape[1]
    out = dot(left2, jnp.concatenate(right_parts, axis=1))
    out = out[:rows] + out[rows:]
    return out[:, :n] + out[:, n:]


def product(left2, right):
    return product_parts(left2, split(right, 2))


def permuted(onehot, x, parts=2):
    n = x.shape[1]
    out = dot(onehot, jnp.concatenate(split(x, parts), axis=1))
    total = out[:, (parts - 1) * n :]
    for i in reversed(range(parts - 1)):
        total = out[:, i * n : (i + 1) * n] + total
    return total


def call(body, out_shapes, scalars, arrays, flops=0, scratch=()):
    smem = pl.BlockSpec(memory_space=pltpu.SMEM)
    vmem = pl.BlockSpec(memory_space=pltpu.VMEM)
    moved = sum(a.size * a.dtype.itemsize for a in arrays)
    return pl.pallas_call(
        body,
        out_shape=[jax.ShapeDtypeStruct(s, d) for s, d in out_shapes],
        in_specs=[smem] * len(scalars) + [vmem] * len(arrays),
        out_specs=[vmem] * len(out_shapes),
        scratch_shapes=[pltpu.VMEM(shape, F32) for shape in scratch],
        compiler_params=pltpu.CompilerParams(vmem_limit_bytes=VMEM_LIMIT),
        cost_estimate=pl.CostEstimate(flops=flops, bytes_accessed=moved, transcendentals=0),
        interpret=INTERPRET,
    )(*scalars, *arrays)


def pack(ref, start, x):
    rows, width = x.shape
    for i in range(0, width, LANES):
        w = min(LANES, width - i)
        ref[start : start + rows, :w] = x[:, i : i + w]
        start += rows
    return start


def unpack(ref, start, rows, width):
    parts = []
    for i in range(0, width, LANES):
        parts.append(ref[start : start + rows, : min(LANES, width - i)])
        start += rows
    return jnp.concatenate(parts, axis=1) if len(parts) > 1 else parts[0]


def blocks(width):
    return -(-width // LANES)


def pack_halves(ref, start, x):
    half = x.shape[0] // 2
    ref[start : start + half, : x.shape[1]] = x[:half]
    ref[start : start + half, LANES // 2 : LANES // 2 + x.shape[1]] = x[half:]


def unpack_halves(ref, start, rows, width):
    x = ref[start : start + rows // 2, :]
    return jnp.concatenate([x[:, :width], x[:, LANES // 2 : LANES // 2 + width]], axis=0)


def transposed(x, pad_ref):
    rows, width = x.shape
    pad_ref[...] = jnp.zeros_like(pad_ref)
    pad_ref[:rows, :width] = x
    return pad_ref[...].T[:width, :rows]


def index_kernel(face, columns, place_ref, index_ref, load_ref, perm_ref, back_ref, load_out):
    size = perm_ref.shape[0]
    raw = index_ref[...].astype(F32)
    west, east, south, north = [raw[:, k * face : (k + 1) * face] for k in range(4)]
    even_row, even_col = place_ref[0] % 2 == 0, place_ref[1] % 2 == 0
    index = jnp.concatenate(
        [
            jnp.where(even_col, east, west),
            jnp.where(even_col, west, east),
            jnp.where(even_row, north, south),
            jnp.where(even_row, south, north),
        ],
        axis=1,
    )
    tall = jnp.broadcast_to(index, (LANES, size)).T
    lane = lax.broadcasted_iota(jnp.int32, (size, LANES), 1).astype(F32)
    for i in range(0, size, LANES):
        perm_ref[:, i : i + LANES] = jnp.where(tall == lane + float(i), 1.0, 0.0).astype(BF16)
    down = lax.broadcasted_iota(jnp.int32, (size, size), 0).astype(F32)
    back_ref[...] = jnp.where(index == down, 1.0, 0.0).astype(BF16)
    load_out[...] = permuted(perm_ref[...], load_ref[:, :columns])


def start_kernel(
    face,
    shapes,
    perm_ref,
    load_ref,
    basis_ref,
    small_in_ref,
    basis_out,
    coarse_out,
    basis2_ref,
    map_t_ref,
    inverse_out,
    top_out,
    e_ref,
    f_ref,
    g_ref,
    h_ref,
    tall_ref,
    small_ref,
):
    coarse, total, top, _ = shapes
    columns = load_ref.shape[1]
    level = small_in_ref[:, : total + top]
    inverse, mapped, tops = level[:, :total], level[:, total:], small_in_ref[:, blocks(total + top) * LANES :]
    basis = permuted(perm_ref[...], basis_ref[:, columns : columns + coarse])
    basis_out[...] = basis
    product_map = product(stack_split(basis), mapped)
    coarse_out[...] = product_map
    inverse_out[...] = inverse
    top_out[...] = tops
    for k, ref in enumerate((e_ref, f_ref, g_ref, h_ref)):
        rows = slice(k * face, (k + 1) * face)
        ref[:face] = load_ref[rows]
        ref[face:] = jnp.zeros((ref.shape[0] - face, ref.shape[1]), F32)
        pack_halves(ref, face, product_map[rows] if k < 2 else basis[rows])
        pack(ref, face + face // 2, tops if k < 2 else level)
    basis2_ref[...] = stack_split(transposed(basis, tall_ref))
    map_t_ref[...] = jnp.zeros_like(map_t_ref)
    map_t_ref[:, :coarse] = transposed(mapped, small_ref)


def fold_kernel(perm_ref, x_ref, *refs):
    rows = x_ref.shape[0]
    for i, part in enumerate(split(x_ref[...], 2)):
        part = dot(perm_ref[...], part).astype(BF16)
        if len(refs) > 1:
            part = dot(part, refs[0][...]).astype(BF16)
        refs[-1][i * rows : (i + 1) * rows] = part


def restore_kernel(x_ref, back_ref, out_ref):
    out_ref[...] = permuted(back_ref[...], x_ref[...], 3)


def level_kernel(
    face, link_ref, order_ref, basis_ref, inverse_ref, coarse_ref, top_ref, e_ref, f_ref, g_ref, h_ref, two_ref, own_ref, far_ref
):
    coarse, total = inverse_ref.shape
    top, width = top_ref.shape
    start = face + face // 2
    link = [link_ref[i].astype(F32) for i in range(4)]
    two = product(stack_split(basis_ref[...]), inverse_ref[...])
    third = coarse_ref[...]
    twos, thirds = [two[: 2 * face]], [third[: 2 * face]]
    for k, ref in ((2, g_ref), (3, h_ref)):
        rows = slice(k * face, (k + 1) * face)
        basis = stack_split(unpack_halves(ref, face, face, coarse) * link[k])
        level = product(basis, unpack(ref, start, coarse, total + top))
        twos.append(two[rows] + level[:, :total])
        thirds.append(third[rows] + level[:, total:])
    two_ref[...] = stack_split(jnp.concatenate(twos, axis=0))
    out = product(stack_split(jnp.concatenate(thirds, axis=0)), top_ref[...])
    outs = []
    for k, ref in ((0, e_ref), (1, f_ref)):
        rows = slice(k * face, (k + 1) * face)
        near = stack_split(unpack_halves(ref, face, face, top) * link[k])
        outs.append(out[rows] + product(near, unpack(ref, start, top, width)))
    out = jnp.concatenate(outs + [out[2 * face :]], axis=0)
    low, high = out[:, : width // 2], out[:, width // 2 :]
    near = order_ref[0] < width // 2
    own_ref[...] = stack_split(jnp.where(near, low, high))
    far_ref[...] = stack_split(jnp.where(near, high, low))


def cross_kernel(schur_ref, far_ref, out_ref):
    rows = far_ref.shape[0] // 2
    parts = [far_ref[:rows], far_ref[rows:]]
    out_ref[:rows], out_ref[2 * rows : 3 * rows] = parts
    hi, lo = split(product_parts(schur_ref[...], parts), 2)
    out_ref[rows : 2 * rows], out_ref[3 * rows :] = hi, lo


def received(face, link_ref, refs):
    return jnp.concatenate([r[:face] * link_ref[i].astype(F32) for i, r in enumerate(refs)], axis=0)


def coeffs_kernel(first, face, link_ref, f_ref, r0, r1, r2, r3, *refs):
    field = f_ref[...] + received(face, link_ref, (r0, r1, r2, r3))
    if first:
        basis_ref, current_ref, c_ref = refs
        current = field
    else:
        asm_ref, basis_ref, current_ref, c_ref = refs
        current = asm_ref[...] - field
    current_ref[...] = current
    c_ref[...] = product(basis_ref[...], current)


def local_kernel(face, current_ref, inverse_ref, back_ref, y_ref, g_ref, h_ref):
    n = current_ref.shape[1]
    moved = dot(back_ref[...], jnp.concatenate(split(current_ref[...], 2), axis=1)).astype(BF16)
    y = product_parts(inverse_ref[...], [moved[:, :n], moved[:, n:]])
    y_ref[...] = y
    g_ref[...] = y[2 * face : 3 * face]
    h_ref[...] = y[3 * face :]


def maps_kernel(coarse, starts, *refs):
    out_ref = refs[-1]
    slot = 0
    for ref, spans in zip(refs, starts):
        for start in spans:
            part = stack_split(ref[start : start + coarse, :coarse])
            out_ref[slot * part.shape[0] : (slot + 1) * part.shape[0]] = part
            slot += 1


def third_kernel(starts, coarse, maps_ref, *refs):
    third, slot = None, 0
    rows = maps_ref.shape[0] // sum(len(spans) for spans in starts)
    for ref, spans in zip(refs, starts):
        for start in spans:
            part = product(maps_ref[slot * rows : (slot + 1) * rows], ref[start : start + coarse])
            third = part if third is None else third + part
            slot += 1
    refs[-1][...] = third


def group_kernel(starts, coarse, order_ref, y_ref, two_ref, *refs):
    y2_ref, stack_ref = refs[len(starts) :]
    slot = 0
    for ref, spans in zip(refs, starts):
        for start in spans:
            offset = pl.multiple_of(order_ref[slot], 8)
            stack_ref[pl.ds(offset, coarse)] = ref[start : start + coarse]
            slot += 1
    y2_ref[...] = y_ref[...] + product(two_ref[...], stack_ref[...])


def stacked(order_ref, slot, top, refs, stack_ref):
    for ref in refs:
        for start in range(0, ref.shape[0], top):
            offset = lax.rem(order_ref[slot], stack_ref.shape[0])
            stack_ref[pl.ds(pl.multiple_of(offset, 8), top)] = ref[start : start + top]
            slot += 1
    return stack_ref[...]


def partial_kernel(weight, face, top, link_ref, order_ref, y2_ref, r0, r1, r2, r3, own_ref, schur_ref, old_ref, *refs):
    x_ref, out_ref, stack_ref = refs[-3:]
    known = stacked(order_ref, 0, top, refs[:-3], stack_ref)
    update = y2_ref[...] + received(face, link_ref, (r0, r1, r2, r3)) + product(own_ref[...], known)
    x = old_ref[...] + weight * update
    x_ref[...] = x
    out_ref[...] = product(schur_ref[...], x)


def finish_kernel(weight, top, slot, order_ref, partial_ref, field_ref, cross_ref, more_ref, x_ref, out_ref, stack_ref):
    rows = partial_ref.shape[0]
    more = weight * product(cross_ref[...], stacked(order_ref, slot, top, [more_ref], stack_ref))
    x_ref[...] = partial_ref[...] + more[:rows]
    out_ref[...] = field_ref[...] + more[rows:]


def update_kernel(
    weight, first, face, top, link_ref, order_ref, y2_ref, r0, r1, r2, r3, own_ref, far_ref, schur_ref, *refs
):
    if not first:
        old_ref, refs = refs[0], refs[1:]
    x_ref, out_ref, stack_ref = refs[-3:]
    slot, half = 0, stack_ref.shape[0] // 2
    for ref in refs[:-3]:
        for start in range(0, ref.shape[0], top):
            side = slot * top // half * half
            offset = side + lax.rem(order_ref[slot], half)
            stack_ref[pl.ds(pl.multiple_of(offset, 8), top)] = ref[start : start + top]
            slot += 1
    update = y2_ref[...] + received(face, link_ref, (r0, r1, r2, r3))
    update = update + product(own_ref[...], stack_ref[:half]) + product(far_ref[...], stack_ref[half:])
    x = weight * update
    if not first:
        x = old_ref[...] + x
    x_ref[...] = x
    out_ref[...] = product(schur_ref[...], x)


def residual_kernel(face, link_ref, f_ref, r0, r1, r2, r3, asm_ref, back_ref, out_ref):
    current = asm_ref[...] - (f_ref[...] + received(face, link_ref, (r0, r1, r2, r3)))
    out_ref[...] = permuted(back_ref[...], current)


def swap_pairs(rows, cols, partner):
    pairs = []
    for r in range(rows):
        for c in range(cols):
            a, b = partner(r, c)
            if not (0 <= a < rows and 0 <= b < cols):
                a, b = (r, c ^ 1) if not 0 <= a < rows else (r ^ 1, c)
            if a < rows and b < cols:
                pairs.append((r * cols + c, a * cols + b))
    return pairs


def odd_neighbour(i):
    return i + 1 if i % 2 else i - 1


def shards(
    load,
    schur,
    local_inverse,
    iface_index,
    face_link,
    coarse_basis,
    coarse_inverse,
    coarse_map,
    top_inverse,
):
    loads, basis = load[0, 0], coarse_basis[0, 0]
    inverse_rows, map_block = coarse_inverse[0], coarse_map[0]
    size, columns = loads.shape
    face = size // 4
    coarse, top = basis.shape[1], map_block.shape[1]
    rows, cols = lax.axis_size("row"), lax.axis_size("col")
    row, col = lax.axis_index("row"), lax.axis_index("col")
    total, width = inverse_rows.shape[1], top_inverse.shape[1]

    place = jnp.stack([row, col])
    side = jnp.arange(4, dtype=jnp.int32)
    parity = jnp.where(side < 2, col, row) & 1
    facing = jnp.where(side < 2, 0, 2) + ((side & 1) ^ parity ^ 1)
    link = jnp.sum(jnp.where(facing[:, None] == side[None, :], face_link[0, 0][None, :], 0), axis=1)

    def swap(x, partner):
        return lax.ppermute(x, ("row", "col"), swap_pairs(rows, cols, partner))

    def swap_even_col(x):
        return swap(x, lambda r, c: (r, c ^ 1))

    def swap_odd_col(x):
        return swap(x, lambda r, c: (r, odd_neighbour(c)))

    def swap_even_row(x):
        return swap(x, lambda r, c: (r ^ 1, c))

    def swap_odd_row(x):
        return swap(x, lambda r, c: (odd_neighbour(r), c))

    def exchange(parts):
        got_f = swap_odd_col(parts[1])
        got_g = swap_even_row(parts[2])
        got_h = swap_odd_row(parts[3])
        got_e = swap_even_col(parts[0])
        return [got_e, got_f, got_g, got_h]

    row_pairs = rows == 4

    def faces(x):
        return [x[i * face : (i + 1) * face] for i in range(4)]

    n = (size, columns)
    common = face + face // 2
    payloads = [common + blocks(width) * top] * 2 + [common + blocks(total + top) * coarse] * 2
    wide = jnp.concatenate([loads, basis], axis=1)
    gap = jnp.zeros((coarse, blocks(total + top) * LANES - total - top), F32)
    small = jnp.concatenate([inverse_rows, map_block, gap, top_inverse], axis=1)
    perm, back, load_f = call(
        functools.partial(index_kernel, face, columns),
        [((size, size), BF16), ((size, size), BF16), (n, F32)],
        [place],
        [iface_index[0], wide],
        flops=4 * size**2 * columns,
    )
    basis_f, coarse_f, basis2, map_t, inverse_rows, top_inverse, *sent = call(
        functools.partial(start_kernel, face, (coarse, total, top, width)),
        [((size, coarse), F32), ((size, top), F32), ((2 * coarse, size), BF16), ((top, columns), F32)]
        + [(inverse_rows.shape, F32), (top_inverse.shape, F32)]
        + [((p, columns), F32) for p in payloads],
        [],
        [perm, load_f, wide, small],
        flops=4 * size**2 * columns,
        scratch=[(size, LANES), (LANES, LANES)],
    )

    def folded(x, *more):
        return call(fold_kernel, [((2 * size, size), BF16)], [], [perm, x, *more], flops=4 * size**3)[0]

    inverse2 = folded(local_inverse[0, 0])
    schur2 = folded(schur[0, 0], back)

    got = exchange(sent)
    doubling = cols & (cols - 1) == 0
    col_order = jnp.arange(cols, dtype=jnp.int32)
    if doubling:
        rest = sum((col_order >> i & 1) for i in range(1, cols.bit_length() - 1))
        col_order = col ^ col_order ^ (rest & 1)
    col_order = col_order * top
    two2, own2, far2 = call(
        functools.partial(level_kernel, face),
        [((2 * size, total), BF16)] + [((2 * size, width // 2), BF16)] * 2,
        [link, col_order],
        [basis_f, inverse_rows, coarse_f, top_inverse] + got,
    )
    cross2 = call(cross_kernel, [((4 * size, width // 2), BF16)], [], [schur2, far2], flops=12 * size**2 * width)[0]

    row_order = jnp.arange(rows, dtype=jnp.int32)
    if row_pairs:
        row_order = row ^ ((row_order & 1) * 2 + row_order // 2)
    row_order = row_order * coarse

    solution, field, assembled, maps = load_f, load_f, None, None
    square = 8 * size * size * columns
    for step_index in range(STEPS):
        phase = step_index % DEGREE
        weight = 1.0 / (1.4 - math.cos(math.pi * (2 * phase + 1) / (2 * DEGREE)))
        first = step_index == 0
        if first:
            operands = [load_f] + got + [basis2]
        else:
            operands = [field] + exchange(faces(field)) + [assembled, basis2]
        current, coeffs = call(
            functools.partial(coeffs_kernel, first, face), [(n, F32), ((coarse, columns), F32)], [link], operands
        )
        if first:
            assembled = current

        known = jnp.concatenate([coeffs, map_t]) if first else coeffs
        if row_pairs:
            got_r = swap(known, lambda r, c: (r ^ 2, c))
        y, face_g, face_h = call(
            functools.partial(local_kernel, face),
            [(n, F32), ((face, columns), F32), ((face, columns), F32)],
            [],
            [current, inverse2, back],
            flops=2 * square,
        )
        if row_pairs:
            got = swap(jnp.concatenate([known, got_r]), lambda r, c: (r ^ 1, c))
            more = known.shape[0]
            pieces, starts = [coeffs, got_r, got], ((0,), (0,), (0, more))
            map_starts, sources = ((0,), (coarse,), (coarse, more + coarse)), [map_t, got_r, got]
        else:
            pieces = [lax.all_gather(coeffs, "row", axis=0, tiled=True)]
            starts = map_starts = (tuple(range(0, total, coarse)),)
            sources = [lax.all_gather(map_t, "row", axis=0, tiled=True)] if first else None
        got_g = swap_even_row(face_g)
        got_h = swap_odd_row(face_h)
        if first:
            maps = call(
                functools.partial(maps_kernel, coarse, map_starts), [((2 * rows * top, coarse), BF16)], [], sources
            )[0]
        third = call(functools.partial(third_kernel, starts, coarse), [((top, columns), F32)], [], [maps] + pieces)[0]

        if doubling:
            more = swap(third, lambda r, c: (r, c ^ 1))
        y2 = call(
            functools.partial(group_kernel, starts, coarse),
            [(n, F32)],
            [row_order],
            [y, two2] + pieces,
            scratch=[(total, columns)],
        )[0]
        got_f = swap_odd_col(y2[face : 2 * face])
        got_e = swap_even_col(y2[:face])
        if doubling:
            tops, bits = [third, more], 2
            known = jnp.concatenate([third, more])
            while bits < cols:
                more = swap(known, lambda r, c: (r, c ^ bits ^ 1))
                tops.append(more)
                known = jnp.concatenate([known, more])
                bits *= 2
        else:
            tops = [lax.all_gather(third, "col", axis=0, tiled=True)]
        out = [y2, got_e, got_f, got_g, got_h]
        if first or not doubling:
            solution, field = call(
                functools.partial(update_kernel, weight, first, face, top),
                [(n, F32), (n, F32)],
                [link, col_order],
                out + [own2, far2, schur2] + ([] if first else [solution]) + tops,
                flops=2 * square,
                scratch=[(width, columns)],
            )
        else:
            solution, field = call(
                functools.partial(partial_kernel, weight, face, top),
                [(n, F32), (n, F32)],
                [link, col_order],
                out + [own2, schur2, solution] + tops[:-1],
                flops=2 * square,
                scratch=[(width // 2, columns)],
            )
            solution, field = call(
                functools.partial(finish_kernel, weight, top, cols // 2),
                [(n, F32), (n, F32)],
                [col_order],
                [solution, field, cross2, tops[-1]],
                flops=square,
                scratch=[(width // 2, columns)],
            )
    solution = call(restore_kernel, [(n, F32)], [], [solution, back], flops=square)[0]
    residual = call(
        functools.partial(residual_kernel, face),
        [(n, F32)],
        [link],
        [field] + exchange(faces(field)) + [assembled, back],
    )[0]
    return (solution[None, None], residual[None, None])


def solution(mesh):
    return jax.shard_map(
        shards,
        mesh=mesh,
        in_specs=(
            P("row", "col", None, None),
            P("row", "col", None, None),
            P("row", "col", None, None),
            P("row", "col", None),
            P("row", "col", None),
            P("row", "col", None, None),
            P("col", "row", None),
            P("col", "row", None),
            P("col", None),
        ),
        out_specs=(P("row", "col", None, None), P("row", "col", None, None)),
        check_vma=False,
    )
```

```python
import functools
import math

import jax
import jax.numpy as jnp
from jax import lax
from jax.experimental import pallas as pl
from jax.experimental.pallas import tpu as pltpu
from jax.sharding import PartitionSpec as P


DEGREE = 2
STEPS = 4
LANES = 128
INTERPRET = False
VMEM_LIMIT = 16 * 2**20
F32 = jnp.float32
BF16 = jnp.bfloat16


def split(x, parts):
    pieces = []
    for _ in range(parts - 1):
        piece = x.astype(BF16)
        pieces.append(piece)
        x = x - piece.astype(F32)
    pieces.append(x.astype(BF16))
    return pieces


def stack_split(x):
    return jnp.concatenate(split(x, 2), axis=0)


def dot(left, right):
    return jnp.dot(left, right, preferred_element_type=F32)


def product_parts(left2, right_parts):
    rows = left2.shape[0] // 2
    n = right_parts[0].shape[1]
    high = dot(left2[:rows], jnp.concatenate(right_parts, axis=1))
    return high[:, :n] + (high[:, n:] + dot(left2[rows:], right_parts[0]))


def product(left2, right):
    return product_parts(left2, split(right, 2))


def permuted(onehot, x, parts=2):
    n = x.shape[1]
    out = dot(onehot, jnp.concatenate(split(x, parts), axis=1))
    total = out[:, (parts - 1) * n :]
    for i in reversed(range(parts - 1)):
        total = out[:, i * n : (i + 1) * n] + total
    return total


def call(body, out_shapes, scalars, arrays, flops=0, scratch=()):
    smem = pl.BlockSpec(memory_space=pltpu.SMEM)
    vmem = pl.BlockSpec(memory_space=pltpu.VMEM)
    moved = sum(a.size * a.dtype.itemsize for a in arrays)
    return pl.pallas_call(
        body,
        out_shape=[jax.ShapeDtypeStruct(s, d) for s, d in out_shapes],
        in_specs=[smem] * len(scalars) + [vmem] * len(arrays),
        out_specs=[vmem] * len(out_shapes),
        scratch_shapes=[pltpu.VMEM(shape, F32) for shape in scratch],
        compiler_params=pltpu.CompilerParams(vmem_limit_bytes=VMEM_LIMIT),
        cost_estimate=pl.CostEstimate(flops=flops, bytes_accessed=moved, transcendentals=0),
        interpret=INTERPRET,
    )(*scalars, *arrays)


def pack(ref, start, x):
    rows, width = x.shape
    for i in range(0, width, LANES):
        w = min(LANES, width - i)
        ref[start : start + rows, :w] = x[:, i : i + w]
        start += rows
    return start


def unpack(ref, start, rows, width):
    parts = []
    for i in range(0, width, LANES):
        parts.append(ref[start : start + rows, : min(LANES, width - i)])
        start += rows
    return jnp.concatenate(parts, axis=1) if len(parts) > 1 else parts[0]


def blocks(width):
    return -(-width // LANES)


def pack_halves(ref, start, x):
    half = x.shape[0] // 2
    ref[start : start + half, : x.shape[1]] = x[:half]
    ref[start : start + half, LANES // 2 : LANES // 2 + x.shape[1]] = x[half:]


def unpack_halves(ref, start, rows, width):
    x = ref[start : start + rows // 2, :]
    return jnp.concatenate([x[:, :width], x[:, LANES // 2 : LANES // 2 + width]], axis=0)


def transposed(x, pad_ref):
    rows, width = x.shape
    pad_ref[...] = jnp.zeros_like(pad_ref)
    pad_ref[:rows, :width] = x
    return pad_ref[...].T[:width, :rows]


def index_kernel(face, columns, place_ref, index_ref, load_ref, perm_ref, back_ref, load_out):
    size = perm_ref.shape[0]
    raw = index_ref[...].astype(F32)
    west, east, south, north = [raw[:, k * face : (k + 1) * face] for k in range(4)]
    even_row, even_col = place_ref[0] % 2 == 0, place_ref[1] % 2 == 0
    index = jnp.concatenate(
        [
            jnp.where(even_col, east, west),
            jnp.where(even_col, west, east),
            jnp.where(even_row, north, south),
            jnp.where(even_row, south, north),
        ],
        axis=1,
    )
    tall = jnp.broadcast_to(index, (LANES, size)).T
    lane = lax.broadcasted_iota(jnp.int32, (size, LANES), 1).astype(F32)
    for i in range(0, size, LANES):
        perm_ref[:, i : i + LANES] = jnp.where(tall == lane + float(i), 1.0, 0.0).astype(BF16)
    down = lax.broadcasted_iota(jnp.int32, (size, size), 0).astype(F32)
    back_ref[...] = jnp.where(index == down, 1.0, 0.0).astype(BF16)
    load_out[...] = permuted(perm_ref[...], load_ref[:, :columns])


def start_kernel(
    face,
    shapes,
    perm_ref,
    load_ref,
    basis_ref,
    small_in_ref,
    basis_out,
    coarse_out,
    basis2_ref,
    map_t_ref,
    inverse_out,
    top_out,
    e_ref,
    f_ref,
    g_ref,
    h_ref,
    tall_ref,
    small_ref,
):
    coarse, total, top, _ = shapes
    columns = load_ref.shape[1]
    level = small_in_ref[:, : total + top]
    inverse, mapped, tops = level[:, :total], level[:, total:], small_in_ref[:, blocks(total + top) * LANES :]
    basis = permuted(perm_ref[...], basis_ref[:, columns : columns + coarse])
    basis_out[...] = basis
    product_map = product(stack_split(basis), mapped)
    coarse_out[...] = product_map
    inverse_out[...] = inverse
    top_out[...] = tops
    for k, ref in enumerate((e_ref, f_ref, g_ref, h_ref)):
        rows = slice(k * face, (k + 1) * face)
        ref[:face] = load_ref[rows]
        ref[face:] = jnp.zeros((ref.shape[0] - face, ref.shape[1]), F32)
        pack_halves(ref, face, product_map[rows] if k < 2 else basis[rows])
        pack(ref, face + face // 2, tops if k < 2 else level)
    basis2_ref[...] = stack_split(transposed(basis, tall_ref))
    map_t_ref[...] = jnp.zeros_like(map_t_ref)
    map_t_ref[:, :coarse] = transposed(mapped, small_ref)


def fold_kernel(perm_ref, x_ref, *refs):
    rows = x_ref.shape[0]
    for i, part in enumerate(split(x_ref[...], 2)):
        part = dot(perm_ref[...], part).astype(BF16)
        if len(refs) > 1:
            part = dot(part, refs[0][...]).astype(BF16)
        refs[-1][i * rows : (i + 1) * rows] = part


def restore_kernel(x_ref, back_ref, out_ref):
    out_ref[...] = permuted(back_ref[...], x_ref[...], 3)


def level_kernel(
    face, link_ref, order_ref, basis_ref, inverse_ref, coarse_ref, top_ref, e_ref, f_ref, g_ref, h_ref, two_ref, own_ref, far_ref
):
    coarse, total = inverse_ref.shape
    top, width = top_ref.shape
    start = face + face // 2
    link = [link_ref[i].astype(F32) for i in range(4)]
    two = product(stack_split(basis_ref[...]), inverse_ref[...])
    third = coarse_ref[...]
    twos, thirds = [two[: 2 * face]], [third[: 2 * face]]
    for k, ref in ((2, g_ref), (3, h_ref)):
        rows = slice(k * face, (k + 1) * face)
        basis = stack_split(unpack_halves(ref, face, face, coarse) * link[k])
        level = product(basis, unpack(ref, start, coarse, total + top))
        twos.append(two[rows] + level[:, :total])
        thirds.append(third[rows] + level[:, total:])
    two_ref[...] = stack_split(jnp.concatenate(twos, axis=0))
    out = product(stack_split(jnp.concatenate(thirds, axis=0)), top_ref[...])
    outs = []
    for k, ref in ((0, e_ref), (1, f_ref)):
        rows = slice(k * face, (k + 1) * face)
        near = stack_split(unpack_halves(ref, face, face, top) * link[k])
        outs.append(out[rows] + product(near, unpack(ref, start, top, width)))
    out = jnp.concatenate(outs + [out[2 * face :]], axis=0)
    low, high = out[:, : width // 2], out[:, width // 2 :]
    near = order_ref[0] < width // 2
    own_ref[...] = stack_split(jnp.where(near, low, high))
    far_ref[...] = stack_split(jnp.where(near, high, low))


def cross_kernel(schur_ref, far_ref, out_ref):
    rows = far_ref.shape[0] // 2
    parts = [far_ref[:rows], far_ref[rows:]]
    out_ref[:rows], out_ref[2 * rows : 3 * rows] = parts
    hi, lo = split(product_parts(schur_ref[...], parts), 2)
    out_ref[rows : 2 * rows], out_ref[3 * rows :] = hi, lo


def received(face, link_ref, refs):
    return jnp.concatenate([r[:face] * link_ref[i].astype(F32) for i, r in enumerate(refs)], axis=0)


def coeffs_kernel(first, face, link_ref, f_ref, r0, r1, r2, r3, *refs):
    field = f_ref[...] + received(face, link_ref, (r0, r1, r2, r3))
    if first:
        basis_ref, current_ref, c_ref = refs
        current = field
    else:
        asm_ref, basis_ref, current_ref, c_ref = refs
        current = asm_ref[...] - field
    current_ref[...] = current
    c_ref[...] = product(basis_ref[...], current)


def local_kernel(face, current_ref, inverse_ref, back_ref, y_ref, g_ref, h_ref):
    n = current_ref.shape[1]
    moved = dot(back_ref[...], jnp.concatenate(split(current_ref[...], 2), axis=1)).astype(BF16)
    y = product_parts(inverse_ref[...], [moved[:, :n], moved[:, n:]])
    y_ref[...] = y
    g_ref[...] = y[2 * face : 3 * face]
    h_ref[...] = y[3 * face :]


def maps_kernel(coarse, starts, *refs):
    out_ref = refs[-1]
    slot = 0
    for ref, spans in zip(refs, starts):
        for start in spans:
            part = stack_split(ref[start : start + coarse, :coarse])
            out_ref[slot * part.shape[0] : (slot + 1) * part.shape[0]] = part
            slot += 1


def third_kernel(starts, coarse, maps_ref, *refs):
    third, slot = None, 0
    rows = maps_ref.shape[0] // sum(len(spans) for spans in starts)
    for ref, spans in zip(refs, starts):
        for start in spans:
            part = product(maps_ref[slot * rows : (slot + 1) * rows], ref[start : start + coarse])
            third = part if third is None else third + part
            slot += 1
    refs[-1][...] = third


def group_kernel(starts, coarse, order_ref, y_ref, two_ref, *refs):
    y2_ref, stack_ref = refs[len(starts) :]
    slot = 0
    for ref, spans in zip(refs, starts):
        for start in spans:
            offset = pl.multiple_of(order_ref[slot], 8)
            stack_ref[pl.ds(offset, coarse)] = ref[start : start + coarse]
            slot += 1
    y2_ref[...] = y_ref[...] + product(two_ref[...], stack_ref[...])


def stacked(order_ref, slot, top, refs, stack_ref):
    for ref in refs:
        for start in range(0, ref.shape[0], top):
            offset = lax.rem(order_ref[slot], stack_ref.shape[0])
            stack_ref[pl.ds(pl.multiple_of(offset, 8), top)] = ref[start : start + top]
            slot += 1
    return stack_ref[...]


def partial_kernel(weight, face, top, link_ref, order_ref, y2_ref, r0, r1, r2, r3, own_ref, schur_ref, old_ref, *refs):
    x_ref, out_ref, stack_ref = refs[-3:]
    known = stacked(order_ref, 0, top, refs[:-3], stack_ref)
    update = y2_ref[...] + received(face, link_ref, (r0, r1, r2, r3)) + product(own_ref[...], known)
    x = old_ref[...] + weight * update
    x_ref[...] = x
    out_ref[...] = product(schur_ref[...], x)


def finish_kernel(weight, top, slot, order_ref, partial_ref, field_ref, cross_ref, more_ref, x_ref, out_ref, stack_ref):
    rows = partial_ref.shape[0]
    more = weight * product(cross_ref[...], stacked(order_ref, slot, top, [more_ref], stack_ref))
    x_ref[...] = partial_ref[...] + more[:rows]
    out_ref[...] = field_ref[...] + more[rows:]


def update_kernel(
    weight, first, face, top, link_ref, order_ref, y2_ref, r0, r1, r2, r3, own_ref, far_ref, schur_ref, *refs
):
    if not first:
        old_ref, refs = refs[0], refs[1:]
    x_ref, out_ref, stack_ref = refs[-3:]
    slot, half = 0, stack_ref.shape[0] // 2
    for ref in refs[:-3]:
        for start in range(0, ref.shape[0], top):
            side = slot * top // half * half
            offset = side + lax.rem(order_ref[slot], half)
            stack_ref[pl.ds(pl.multiple_of(offset, 8), top)] = ref[start : start + top]
            slot += 1
    update = y2_ref[...] + received(face, link_ref, (r0, r1, r2, r3))
    update = update + product(own_ref[...], stack_ref[:half]) + product(far_ref[...], stack_ref[half:])
    x = weight * update
    if not first:
        x = old_ref[...] + x
    x_ref[...] = x
    out_ref[...] = product(schur_ref[...], x)


def residual_kernel(face, link_ref, f_ref, r0, r1, r2, r3, asm_ref, back_ref, out_ref):
    current = asm_ref[...] - (f_ref[...] + received(face, link_ref, (r0, r1, r2, r3)))
    out_ref[...] = permuted(back_ref[...], current)


def swap_pairs(rows, cols, partner):
    pairs = []
    for r in range(rows):
        for c in range(cols):
            a, b = partner(r, c)
            if not (0 <= a < rows and 0 <= b < cols):
                a, b = (r, c ^ 1) if not 0 <= a < rows else (r ^ 1, c)
            if a < rows and b < cols:
                pairs.append((r * cols + c, a * cols + b))
    return pairs


def odd_neighbour(i):
    return i + 1 if i % 2 else i - 1


def shards(
    load,
    schur,
    local_inverse,
    iface_index,
    face_link,
    coarse_basis,
    coarse_inverse,
    coarse_map,
    top_inverse,
):
    loads, basis = load[0, 0], coarse_basis[0, 0]
    inverse_rows, map_block = coarse_inverse[0], coarse_map[0]
    size, columns = loads.shape
    face = size // 4
    coarse, top = basis.shape[1], map_block.shape[1]
    rows, cols = lax.axis_size("row"), lax.axis_size("col")
    row, col = lax.axis_index("row"), lax.axis_index("col")
    total, width = inverse_rows.shape[1], top_inverse.shape[1]

    place = jnp.stack([row, col])
    side = jnp.arange(4, dtype=jnp.int32)
    parity = jnp.where(side < 2, col, row) & 1
    facing = jnp.where(side < 2, 0, 2) + ((side & 1) ^ parity ^ 1)
    link = jnp.sum(jnp.where(facing[:, None] == side[None, :], face_link[0, 0][None, :], 0), axis=1)

    def swap(x, partner):
        return lax.ppermute(x, ("row", "col"), swap_pairs(rows, cols, partner))

    def swap_even_col(x):
        return swap(x, lambda r, c: (r, c ^ 1))

    def swap_odd_col(x):
        return swap(x, lambda r, c: (r, odd_neighbour(c)))

    def swap_even_row(x):
        return swap(x, lambda r, c: (r ^ 1, c))

    def swap_odd_row(x):
        return swap(x, lambda r, c: (odd_neighbour(r), c))

    def exchange(parts):
        got_f = swap_odd_col(parts[1])
        got_g = swap_even_row(parts[2])
        got_h = swap_odd_row(parts[3])
        got_e = swap_even_col(parts[0])
        return [got_e, got_f, got_g, got_h]

    row_pairs = rows == 4

    def faces(x):
        return [x[i * face : (i + 1) * face] for i in range(4)]

    n = (size, columns)
    common = face + face // 2
    payloads = [common + blocks(width) * top] * 2 + [common + blocks(total + top) * coarse] * 2
    wide = jnp.concatenate([loads, basis], axis=1)
    gap = jnp.zeros((coarse, blocks(total + top) * LANES - total - top), F32)
    small = jnp.concatenate([inverse_rows, map_block, gap, top_inverse], axis=1)
    perm, back, load_f = call(
        functools.partial(index_kernel, face, columns),
        [((size, size), BF16), ((size, size), BF16), (n, F32)],
        [place],
        [iface_index[0], wide],
        flops=4 * size**2 * columns,
    )
    basis_f, coarse_f, basis2, map_t, inverse_rows, top_inverse, *sent = call(
        functools.partial(start_kernel, face, (coarse, total, top, width)),
        [((size, coarse), F32), ((size, top), F32), ((2 * coarse, size), BF16), ((top, columns), F32)]
        + [(inverse_rows.shape, F32), (top_inverse.shape, F32)]
        + [((p, columns), F32) for p in payloads],
        [],
        [perm, load_f, wide, small],
        flops=4 * size**2 * columns,
        scratch=[(size, LANES), (LANES, LANES)],
    )

    def folded(x, *more):
        return call(fold_kernel, [((2 * size, size), BF16)], [], [perm, x, *more], flops=4 * size**3)[0]

    inverse2 = folded(local_inverse[0, 0])
    schur2 = folded(schur[0, 0], back)

    got = exchange(sent)
    doubling = cols & (cols - 1) == 0
    col_order = jnp.arange(cols, dtype=jnp.int32)
    if doubling:
        rest = sum((col_order >> i & 1) for i in range(1, cols.bit_length() - 1))
        col_order = col ^ col_order ^ (rest & 1)
    col_order = col_order * top
    two2, own2, far2 = call(
        functools.partial(level_kernel, face),
        [((2 * size, total), BF16)] + [((2 * size, width // 2), BF16)] * 2,
        [link, col_order],
        [basis_f, inverse_rows, coarse_f, top_inverse] + got,
    )
    cross2 = call(cross_kernel, [((4 * size, width // 2), BF16)], [], [schur2, far2], flops=12 * size**2 * width)[0]

    row_order = jnp.arange(rows, dtype=jnp.int32)
    if row_pairs:
        row_order = row ^ ((row_order & 1) * 2 + row_order // 2)
    row_order = row_order * coarse

    solution, field, assembled, maps = load_f, load_f, None, None
    square = 8 * size * size * columns
    for step_index in range(STEPS):
        phase = step_index % DEGREE
        weight = 1.0 / (1.4 - math.cos(math.pi * (2 * phase + 1) / (2 * DEGREE)))
        first = step_index == 0
        if first:
            operands = [load_f] + got + [basis2]
        else:
            operands = [field] + exchange(faces(field)) + [assembled, basis2]
        current, coeffs = call(
            functools.partial(coeffs_kernel, first, face), [(n, F32), ((coarse, columns), F32)], [link], operands
        )
        if first:
            assembled = current

        known = jnp.concatenate([coeffs, map_t]) if first else coeffs
        if row_pairs:
            got_r = swap(known, lambda r, c: (r ^ 2, c))
        y, face_g, face_h = call(
            functools.partial(local_kernel, face),
            [(n, F32), ((face, columns), F32), ((face, columns), F32)],
            [],
            [current, inverse2, back],
            flops=2 * square,
        )
        if row_pairs:
            got = swap(jnp.concatenate([known, got_r]), lambda r, c: (r ^ 1, c))
            more = known.shape[0]
            pieces, starts = [coeffs, got_r, got], ((0,), (0,), (0, more))
            map_starts, sources = ((0,), (coarse,), (coarse, more + coarse)), [map_t, got_r, got]
        else:
            pieces = [lax.all_gather(coeffs, "row", axis=0, tiled=True)]
            starts = map_starts = (tuple(range(0, total, coarse)),)
            sources = [lax.all_gather(map_t, "row", axis=0, tiled=True)] if first else None
        got_g = swap_even_row(face_g)
        got_h = swap_odd_row(face_h)
        if first:
            maps = call(
                functools.partial(maps_kernel, coarse, map_starts), [((2 * rows * top, coarse), BF16)], [], sources
            )[0]
        third = call(functools.partial(third_kernel, starts, coarse), [((top, columns), F32)], [], [maps] + pieces)[0]

        if doubling:
            more = swap(third, lambda r, c: (r, c ^ 1))
        y2 = call(
            functools.partial(group_kernel, starts, coarse),
            [(n, F32)],
            [row_order],
            [y, two2] + pieces,
            scratch=[(total, columns)],
        )[0]
        got_f = swap_odd_col(y2[face : 2 * face])
        got_e = swap_even_col(y2[:face])
        if doubling:
            tops, bits = [third, more], 2
            known = jnp.concatenate([third, more])
            while bits < cols:
                more = swap(known, lambda r, c: (r, c ^ bits ^ 1))
                tops.append(more)
                known = jnp.concatenate([known, more])
                bits *= 2
        else:
            tops = [lax.all_gather(third, "col", axis=0, tiled=True)]
        out = [y2, got_e, got_f, got_g, got_h]
        if first or not doubling:
            solution, field = call(
                functools.partial(update_kernel, weight, first, face, top),
                [(n, F32), (n, F32)],
                [link, col_order],
                out + [own2, far2, schur2] + ([] if first else [solution]) + tops,
                flops=2 * square,
                scratch=[(width, columns)],
            )
        else:
            solution, field = call(
                functools.partial(partial_kernel, weight, face, top),
                [(n, F32), (n, F32)],
                [link, col_order],
                out + [own2, schur2, solution] + tops[:-1],
                flops=2 * square,
                scratch=[(width // 2, columns)],
            )
            solution, field = call(
                functools.partial(finish_kernel, weight, top, cols // 2),
                [(n, F32), (n, F32)],
                [col_order],
                [solution, field, cross2, tops[-1]],
                flops=square,
                scratch=[(width // 2, columns)],
            )
    solution = call(restore_kernel, [(n, F32)], [], [solution, back], flops=square)[0]
    residual = call(
        functools.partial(residual_kernel, face),
        [(n, F32)],
        [link],
        [field] + exchange(faces(field)) + [assembled, back],
    )[0]
    return (solution[None, None], residual[None, None])


def solution(mesh):
    return jax.shard_map(
        shards,
        mesh=mesh,
        in_specs=(
            P("row", "col", None, None),
            P("row", "col", None, None),
            P("row", "col", None, None),
            P("row", "col", None),
            P("row", "col", None),
            P("row", "col", None, None),
            P("col", "row", None),
            P("col", "row", None),
            P("col", None),
        ),
        out_specs=(P("row", "col", None, None), P("row", "col", None, None)),
        check_vma=False,
    )
```
